256 devices in a mesh: seq: 16 (over z, y_lo), res: 16 (over x, y_hi, core).
Axes of the slice: x: 4, y: 4 (y_hi: 2, y_lo: 2; y = y_hi * 2 + y_lo), z: 8, core: 2. Of those that a mesh axis runs over, the one named last changes fastest.
Arguments:
- alignment_embedding: bfloat16 [256, 512, 768], P('seq', 'res'), may hold values from -12 to 12
- probe_projector: bfloat16 [768, 768], replicated, may hold values from -0.21875 to 0.21875
- lookup_projector: bfloat16 [768, 768], replicated, may hold values from -0.21875 to 0.21875
- content_projector: bfloat16 [768, 768], replicated, may hold values from -0.21875 to 0.21875
- final_projector: bfloat16 [768, 768], replicated, may hold values from -0.21875 to 0.21875
Outputs:
- mixed: bfloat16 [256, 512, 768], P('seq', 'res')
The draws below stay inside these ranges and needn't reach their ends.
All inputs are finite; a program needn't handle non-finite values.
Results may differ from the reference program's by a relative error of at most 0.01.
Values may be sent and summed in bfloat16 or wider, within the bound.
A program may use at most 128 MiB of HBM per device.

```python
import jax
import jax.numpy as jnp
from jax import lax

EMBED_DIM = 768
H = 12
LOCAL_SEQUENCES = 16
R = 256
ALIGNED_SITES = 512
N_SEQ = 16


def draw_alignment_embedding(key, part):
    base = jax.random.normal(jax.random.fold_in(key, 11), (R, ALIGNED_SITES, EMBED_DIM), jnp.float32)
    base = jnp.clip(base, -6.0, 6.0)
    return jnp.clip(base, -12.0, 12.0).astype(jnp.bfloat16)


def centred(key, extent, deviation, limit, dtype=jnp.bfloat16):
    entries = deviation * jax.random.normal(key, extent, jnp.float32)
    return jnp.clip(entries, min=-limit, max=limit).astype(dtype)


def setup_inputs(seed: int = 0) -> dict:
    key_of = jax.random.split(jax.random.key(seed), 6)
    alignment_embedding = draw_alignment_embedding(jax.random.fold_in(key_of[5], 71), 0)
    probe_projector = centred(key_of[1], (EMBED_DIM, EMBED_DIM), EMBED_DIM ** -0.5, 0.21875)
    lookup_projector = centred(key_of[2], (EMBED_DIM, EMBED_DIM), EMBED_DIM ** -0.5, 0.21875)
    content_projector = centred(key_of[3], (EMBED_DIM, EMBED_DIM), EMBED_DIM ** -0.5, 0.21875)
    final_projector = centred(key_of[4], (EMBED_DIM, EMBED_DIM), EMBED_DIM ** -0.5, 0.21875)
    return dict(alignment_embedding=alignment_embedding, probe_projector=probe_projector, lookup_projector=lookup_projector, content_projector=content_projector, final_projector=final_projector)


def project(block, weight):
    flat = block.reshape(-1, EMBED_DIM)
    out = jnp.dot(flat, weight, preferred_element_type=jnp.float32).astype(jnp.bfloat16)
    return out.reshape(block.shape[0], ALIGNED_SITES, H, EMBED_DIM // H)

def reference(alignment_embedding, probe_projector, lookup_projector, content_projector, final_projector):
    tile_groups = alignment_embedding.reshape(N_SEQ, LOCAL_SEQUENCES, ALIGNED_SITES, EMBED_DIM)

    def add_logits(total, block):
        probe_tensor = project(block, probe_projector).astype(jnp.float32)
        lookup_tensor = project(block, lookup_projector).astype(jnp.float32)
        return (total + jnp.einsum('rihe,rjhe->hij', probe_tensor, lookup_tensor), None)
    logits, _ = lax.scan(add_logits, jnp.zeros((H, ALIGNED_SITES, ALIGNED_SITES), jnp.float32), tile_groups)
    logits = logits / jnp.sqrt(jnp.float32(EMBED_DIM // H * R))
    probs = jax.nn.softmax(logits, axis=-1).astype(jnp.bfloat16)

    def finish(block):
        content_tensor = project(block, content_projector).astype(jnp.float32)
        attended = jnp.einsum('hij,rjhe->rihe', probs.astype(jnp.float32), content_tensor).astype(jnp.bfloat16)
        mixed = jnp.dot(attended.reshape(-1, EMBED_DIM), final_projector, preferred_element_type=jnp.float32)
        return mixed.astype(jnp.bfloat16).reshape(LOCAL_SEQUENCES, ALIGNED_SITES, EMBED_DIM)
    return lax.map(finish, tile_groups).reshape(R, ALIGNED_SITES, EMBED_DIM)
```

```python
import math

import jax
import jax.numpy as jnp
from jax import lax
from jax.experimental import pallas as pl
from jax.experimental.pallas import tpu as pltpu
from jax.sharding import PartitionSpec as P

MESH = pl.DeviceIdType.MESH
BF16, F32 = jnp.bfloat16, jnp.float32

H = 12
E = 64
D = 768
ROWS = 16
COLS = 32
NSEQ = 16
HD = D // 2
NP = HD // 128
SITES = 512

O, Y, L, R, YL, YR, OPP, YOPP = range(8)
PARTS = {b: ((0, 5), (5, 4), (9, 3), (12, 4)) for b in range(8)}
PARTS[YOPP] = ((0, 5), (5, 5), (10, 3), (13, 3))
UNIT = 2 * COLS
NZ = 8
OWNED = HD * UNIT // E // NZ
PIECE = OWNED // 2


def kernel(
    x_hbm,
    wq_hbm,
    wk_hbm,
    wv_hbm,
    wo_hbm,
    out_hbm,
    xs,
    wq,
    wkv,
    wo,
    qp,
    kp,
    vp,
    ls,
    lbuf,
    rz,
    sz,
    ry,
    pall,
    factors,
    pfull,
    parts,
    half,
    full,
    in_sem,
    out_sem,
    tx_sem,
    rx_sem,
    mate_sem,
    ltx_sem,
    lrx_sem,
    ytx_sem,
    yrx_sem,
    ptx_sem,
    prx_sem,
    ftx_sem,
    frx_sem,
    htx_sem,
    hrx_sem,
):
    s, r = lax.axis_index("seq"), lax.axis_index("res")
    z, yl = s // 2, lax.rem(s, 2)
    ix, yh, core = r // 4, lax.rem(r // 2, 2), lax.rem(r, 2)

    def at(dx, dy, dc):
        return (s, lax.rem(ix + dx + 4, 4) * 4 + lax.rem(yh + dy, 2) * 2 + lax.rem(core + dc, 2))

    right, left, across, mate = at(1, 0, 0), at(-1, 0, 0), at(0, 1, 0), at(0, 0, 1)

    def above(d):
        return (lax.rem(z + d, NZ) * 2 + yl, r)

    twin = (z * 2 + 1 - yl, r)

    barrier = pltpu.get_barrier_semaphore()
    for device in (right, left, across, mate, twin, *(above(d) for d in range(1, NZ))):
        pl.semaphore_signal(barrier, inc=1, device_id=device, device_id_type=MESH)

    mine = pl.ds(pl.multiple_of(core * HD, HD), HD)
    others = pl.ds(pl.multiple_of((1 - core) * HD, HD), HD)
    loads = [
        pltpu.make_async_copy(x_hbm, xs.at[O, 0], in_sem.at[0]),
        pltpu.make_async_copy(wq_hbm.at[:, mine], wq, in_sem.at[1]),
        pltpu.make_async_copy(wk_hbm.at[:, mine], wkv.at[:, pl.ds(0, HD)], in_sem.at[2]),
        pltpu.make_async_copy(wv_hbm.at[:, mine], wkv.at[:, pl.ds(HD, HD)], in_sem.at[3]),
        pltpu.make_async_copy(wo_hbm.at[mine, :], wo.at[pl.ds(0, HD)], in_sem.at[4]),
        pltpu.make_async_copy(wo_hbm.at[others, :], wo.at[pl.ds(HD, HD)], in_sem.at[5]),
    ]
    for copy in loads:
        copy.start()
    pl.semaphore_wait(barrier, 5 + NZ - 1)

    def send(block, part, device, landing):
        rows = pl.ds(*PARTS[landing][part])
        pltpu.make_async_remote_copy(
            src_ref=x_hbm.at[rows] if block == O else xs.at[block, 0, rows],
            dst_ref=xs.at[landing, 0, rows],
            send_sem=tx_sem.at[0],
            recv_sem=rx_sem.at[landing, part],
            device_id=device,
            device_id_type=MESH,
        ).start()

    def hand_on(block, part):
        rows = pl.ds(*PARTS[block][part])
        pltpu.make_async_remote_copy(
            src_ref=x_hbm.at[rows] if block == O else xs.at[block, 0, rows],
            dst_ref=xs.at[block, 1, rows],
            send_sem=tx_sem.at[1],
            recv_sem=mate_sem.at[block, part // 2],
            device_id=mate,
            device_id_type=MESH,
        ).start()

    def received(ref, recv_sem):
        return pltpu.make_async_remote_copy(
            src_ref=ref,
            dst_ref=ref,
            send_sem=tx_sem.at[0],
            recv_sem=recv_sem,
            device_id=mate,
            device_id_type=MESH,
        )

    def take(block, *parts):
        for part in parts:
            received(xs.at[block, 0, pl.ds(*PARTS[block][part])], rx_sem.at[block, part]).wait_recv()
            hand_on(block, part)

    def from_mate(block, *halves):
        for side in halves or (0, 1):
            (first, some), (_, more) = PARTS[block][2 * side : 2 * side + 2]
            ref = xs.at[block, 1, pl.ds(first, some + more)]
            received(ref, mate_sem.at[block, side]).wait_recv()

    def project_rows(block, cr, first, rows, pairs):
        x = xs[block, cr, pl.ds(first, rows)].reshape(rows * COLS, D)
        w = wkv[:, pl.ds(pairs[0] * 128, len(pairs) * 128)]
        y = jnp.dot(x, w, preferred_element_type=F32).astype(BF16)
        j = pl.ds(pl.multiple_of((2 * block + cr) * COLS, COLS), COLS)
        for row in range(rows):
            lanes = pl.ds((first + row) * 128, 128)
            for n, pair in enumerate(pairs):
                here = y[row * COLS : (row + 1) * COLS, n * 128 : (n + 1) * 128]
                if pair < NP:
                    kp[pair, j, lanes] = here
                else:
                    vp[pair - NP, j, lanes] = here

    def project_kv(block, pairs=range(2 * NP)):
        def one(cr, _):
            project_rows(block, cr, 0, ROWS, pairs)
            return 0

        lax.fori_loop(0, 2, one, 0)

    early, late = range(0, NP + 1), range(NP + 1, 2 * NP)

    def project_part(block, cr, side):
        (first, some), (_, more) = PARTS[block][2 * side : 2 * side + 2]
        project_rows(block, cr, first, some + more, early)

    def project_q(cr):
        x = xs[O, cr].reshape(ROWS * COLS, D)
        y = jnp.dot(x, wq[...], preferred_element_type=F32).astype(BF16)
        low = lax.broadcasted_iota(jnp.int32, (COLS, 128), 1) < E
        zero = jnp.zeros((COLS, 128), BF16)
        for row in range(ROWS):
            for pair in range(NP):
                q = y[row * COLS : (row + 1) * COLS, pair * 128 : (pair + 1) * 128]
                lanes = pl.ds(row * 128, 128)
                qp[pair, pl.ds(cr * COLS, COLS), lanes] = jnp.where(low, q, zero)
                qp[pair, pl.ds(2 * COLS + cr * COLS, COLS), lanes] = jnp.where(low, zero, q)

    low = lax.broadcasted_iota(jnp.int32, (PIECE, 128), 1) < UNIT

    def logits(unit):
        for pair in range(NP):
            k = kp[pair, pl.ds(unit * UNIT, UNIT), :]
            lbuf[pl.ds(pair * 128, 128), :] = lax.dot_general(
                qp[pair],
                jnp.concatenate([k, k], axis=0),
                (((1,), (1,)), ((), ())),
                preferred_element_type=F32,
            )
        for owner in range(NZ):
            ls[unit, owner] = jnp.where(
                low,
                lbuf[pl.ds(owner * OWNED, PIECE), :],
                lbuf[pl.ds(owner * OWNED + PIECE, PIECE), :],
            )

        def along_z(d, _):
            to = lax.rem(z + d, NZ)
            pltpu.make_async_remote_copy(
                src_ref=ls.at[unit, to],
                dst_ref=rz.at[unit, z],
                send_sem=ltx_sem,
                recv_sem=lrx_sem.at[unit],
                device_id=(to * 2 + yl, r),
                device_id_type=MESH,
            ).start()
            return 0

        lax.fori_loop(1, NZ, along_z, 0)
        rz[unit, z] = ls[unit, z]

    scale = 1.0 / math.sqrt(E * ROWS * NSEQ)

    def group(ref, send_sem, recv_sem):
        return pltpu.make_async_remote_copy(
            src_ref=ref,
            dst_ref=ref,
            send_sem=send_sem,
            recv_sem=recv_sem,
            device_id=mate,
            device_id_type=MESH,
        )

    def fold(unit):
        group(rz.at[unit, pl.ds(0, NZ - 1)], ltx_sem, lrx_sem.at[unit]).wait_recv()
        sz[unit] = jnp.sum(rz[unit], axis=0)
        pltpu.make_async_remote_copy(
            src_ref=sz.at[unit],
            dst_ref=ry.at[unit],
            send_sem=ytx_sem,
            recv_sem=yrx_sem.at[unit],
            device_id=twin,
            device_id_type=MESH,
        ).start()

    def halves(reduce, x, fill):
        first = reduce(jnp.where(low, x, fill), axis=1, keepdims=True)
        second = reduce(jnp.where(low, fill, x), axis=1, keepdims=True)
        return jnp.where(low, first, second)

    def scores_of(unit):
        group(ry.at[unit], ytx_sem, yrx_sem.at[unit]).wait_recv()
        return (sz[unit] + ry[unit]) * scale

    stats = []

    def absorb(*units):
        scores = [scores_of(unit) for unit in units]
        top = scores[0]
        for other in scores[1:]:
            top = jnp.maximum(top, other)
        top = halves(jnp.max, top, -jnp.inf)
        total = jnp.zeros((PIECE, 128), F32)
        for unit, score in zip(units, scores):
            weights = jnp.exp(score - top)
            total = total + weights
            pall[z, unit] = weights.astype(BF16)
        stats.append((top, halves(jnp.sum, total, 0.0)))

    def to_line(ref, send_sem, recv_sem):
        def one(d, _):
            pltpu.make_async_remote_copy(
                src_ref=ref,
                dst_ref=ref,
                send_sem=send_sem,
                recv_sem=recv_sem,
                device_id=above(d),
                device_id_type=MESH,
            ).start()
            return 0

        lax.fori_loop(1, NZ, one, 0)

    def spread(first, count, number):
        to_line(pall.at[z, pl.ds(first, count)], ptx_sem, prx_sem.at[number])

    def shared(first, count, number):
        ref = pall.at[pl.ds(0, NZ - 1), pl.ds(first, count)]
        group(ref, ptx_sem, prx_sem.at[number]).wait_recv()

    lane = lax.broadcasted_iota(jnp.int32, (PIECE, 128), 1)
    row_of = lax.broadcasted_iota(jnp.int32, (PIECE, 128), 0)

    def finish(unit):
        scores = scores_of(unit)
        top = halves(jnp.max, scores, -jnp.inf)
        for earlier, _ in stats:
            top = jnp.maximum(top, earlier)
        weights = jnp.exp(scores - top)
        total = halves(jnp.sum, weights, 0.0)
        scales = [jnp.exp(earlier - top) for earlier, _ in stats]
        for earlier, (_, part) in zip(scales, stats):
            total = total + earlier * part
        pall[z, unit] = (weights / total).astype(BF16)
        spread(unit, 1, 3)
        placed = jnp.zeros((PIECE, 128), F32)
        for number, earlier in enumerate(scales):
            here = lax.rem(lane, UNIT) == row_of + 32 * number
            placed = jnp.where(here, earlier / total, placed)
        factors[z] = jnp.sum(placed, axis=0, keepdims=True)
        to_line(factors.at[z], ftx_sem, frx_sem)

    def unpack(left_unit, right_unit, tile):
        even, odd = (
            pall[:, u].astype(F32).reshape(NZ * PIECE, 128) for u in (left_unit, right_unit)
        )
        wide = lax.broadcasted_iota(jnp.int32, (NZ * PIECE, 128), 1) < UNIT
        first = jnp.where(wide, even, pltpu.roll(odd, UNIT, 1))
        second = jnp.where(wide, pltpu.roll(even, UNIT, 1), odd)
        lanes = pl.ds(tile * 128, 128)
        for n, rows in enumerate((first, second)):
            pfull[:, pl.ds(n * PIECE, PIECE), lanes] = rows.astype(BF16).reshape(NZ, PIECE, 128)

    def factor(number):
        l = lax.broadcasted_iota(jnp.int32, (OWNED, 128), 1)
        i = lax.broadcasted_iota(jnp.int32, (OWNED, 128), 0)
        at_lane = jnp.where(i < PIECE, i, i - PIECE + UNIT) + 32 * number
        row = jnp.broadcast_to(factors[...], (NZ, OWNED, 128))
        return jnp.sum(jnp.where((l == at_lane)[None], row, 0.0), axis=2, keepdims=True)

    first_head = lax.broadcasted_iota(jnp.int32, (2 * COLS, 128), 1) < E

    def by_head(x):
        return jnp.where(first_head, x[: 2 * COLS], x[2 * COLS :])

    def product(pair, tile, first, count):
        probs = pfull[:, :, pl.ds(tile * 128, -(-count // 128) * 128)].reshape(NP * 128, -1)
        probs = probs[pair * 128 : (pair + 1) * 128, :count]
        return jnp.dot(probs, vp[pair, pl.ds(first, count), :], preferred_element_type=F32)

    def attend(number, tile, first, count):
        for pair in range(NP):
            whole = product(pair, tile, first, count)
            for row in range(ROWS):
                cut = slice(row * 128, (row + 1) * 128)
                parts[number, pair, :, cut] = by_head(whole[:, cut])

    for part in (2, 3, 0, 1):
        send(O, part, right, L)
    for part in (3, 2, 1, 0):
        send(O, part, left, R)
    for part in range(4):
        send(O, part, across, Y)
    for part in range(4):
        hand_on(O, part)

    for copy in loads[:4]:
        copy.wait()
    project_q(0)
    from_mate(O)
    project_q(1)
    project_kv(O)
    take(L, 2)
    send(L, 2, right, OPP)
    take(R, 3)
    send(R, 3, left, OPP)
    logits(O)
    take(L, 3)
    take(R, 2)
    for part in (2, 3):
        send(L, part, across, YL)
    take(Y, 0, 1)
    for part in (0, 1):
        send(Y, part, right, YL)
    for part in (1, 0):
        send(Y, part, left, YR)
    take(L, 0)
    send(L, 0, right, OPP)
    take(R, 1)
    send(R, 1, left, OPP)
    take(Y, 2)
    take(L, 1)
    take(R, 0)
    take(Y, 3)
    from_mate(L)
    project_kv(L)
    send(R, 2, across, YR)
    logits(L)
    from_mate(R)
    project_kv(R)
    logits(R)
    take(OPP, 2, 3)
    from_mate(Y)
    project_kv(Y)
    logits(Y)
    take(YL, 0)
    send(YL, 0, right, YOPP)
    take(YR, 1, 2)
    send(YR, 1, left, YOPP)
    take(YL, 2, 3)
    fold(O)
    fold(L)
    send(R, 3, across, YR)
    take(YL, 1)
    fold(R)
    take(YR, 0)
    fold(Y)
    for part in (2, 3):
        send(OPP, part, across, YOPP)
    from_mate(YL)
    project_kv(YL)
    logits(YL)
    take(YR, 3)
    take(OPP, 0, 1)
    absorb(O, Y, L, R)
    spread(O, 2, 0)
    from_mate(YR)
    project_kv(YR)
    logits(YR)
    from_mate(OPP)
    project_kv(OPP)
    logits(OPP)
    take(YOPP, 2, 3)
    project_part(YOPP, 0, 1)
    take(YOPP, 0, 1)
    project_part(YOPP, 0, 0)
    from_mate(YOPP, 1)
    project_part(YOPP, 1, 1)
    from_mate(YOPP, 0)
    project_part(YOPP, 1, 0)
    logits(YOPP)

    spread(L, 2, 1)
    fold(YL)
    fold(YR)
    project_kv(YOPP, late)
    shared(O, 2, 0)
    unpack(O, Y, 0)
    fold(OPP)
    absorb(YL, YR, OPP)
    spread(YL, 3, 2)
    fold(YOPP)
    shared(L, 2, 1)
    unpack(L, R, 1)
    attend(0, 0, O * UNIT, 4 * UNIT)
    finish(YOPP)
    shared(YL, 3, 2)
    unpack(YL, YR, 2)
    unpack(OPP, OPP, 3)
    attend(1, 2, YL * UNIT, 3 * UNIT)
    group(factors.at[pl.ds(0, NZ - 1)], ftx_sem, frx_sem).wait_recv()
    scaling = [factor(number).reshape(NP * 128, 1) for number in range(2)]
    shared(YOPP, 1, 3)
    unpack(YOPP, YOPP, 4)

    handed = []
    for pair in range(NP):
        lanes = pl.ds(pair * 128, 128)
        last = product(pair, 4, YOPP * UNIT, UNIT)
        ranks = [by_head(jnp.broadcast_to(f[pair * 128 : (pair + 1) * 128], (128, 128))) for f in scaling]
        for row in range(ROWS):
            cut = slice(row * 128, (row + 1) * 128)
            picked = by_head(last[:, cut])
            for number, rank in enumerate(ranks):
                picked = picked + rank * parts[number, pair, :, cut]
            picked = picked.astype(BF16)
            full[row, :, lanes] = picked[:COLS]
            half[pair, row] = picked[COLS:]
        copy = pltpu.make_async_remote_copy(
            src_ref=half.at[pair],
            dst_ref=full.at[:, :, pl.ds(HD + pair * 128, 128)],
            send_sem=htx_sem.at[pair],
            recv_sem=hrx_sem.at[pair],
            device_id=mate,
            device_id_type=MESH,
        )
        copy.start()
        handed.append(copy)
    for copy in loads[4:]:
        copy.wait()
    for copy in handed:
        copy.wait_recv()
    stored = []
    for quarter in range(4):
        rows = pl.ds(quarter * 4, 4)
        mixed = jnp.dot(full[rows].reshape(4 * COLS, D), wo[...], preferred_element_type=F32)
        full[rows] = mixed.astype(BF16).reshape(4, COLS, D)
        copy = pltpu.make_async_copy(full.at[rows], out_hbm.at[rows], out_sem.at[quarter])
        copy.start()
        stored.append(copy)

    for count, way in ((7, 0), (8, 1)):
        ref = xs.at[pl.ds(0, count), 0]
        pltpu.make_async_remote_copy(
            src_ref=ref,
            dst_ref=ref,
            send_sem=tx_sem.at[way],
            recv_sem=mate_sem.at[0, 0],
            device_id=mate,
            device_id_type=MESH,
        ).wait_send()
    group(rz.at[:, pl.ds(0, NZ - 1)], ltx_sem, lrx_sem.at[0]).wait_send()
    group(sz, ytx_sem, yrx_sem.at[0]).wait_send()
    group(pall.at[pl.ds(0, NZ - 1)], ptx_sem, prx_sem.at[0]).wait_send()
    group(factors.at[pl.ds(0, NZ - 1)], ftx_sem, frx_sem).wait_send()
    for copy in handed:
        copy.wait_send()
    for copy in stored:
        copy.wait()


def body(alignment_embedding, probe_projector, lookup_projector, content_projector, final_projector):
    hbm = pl.BlockSpec(memory_space=pl.ANY)
    return pl.pallas_call(
        kernel,
        out_shape=jax.ShapeDtypeStruct((ROWS, COLS, D), BF16),
        in_specs=[hbm] * 5,
        out_specs=hbm,
        scratch_shapes=[
            pltpu.VMEM((8, 2, ROWS, COLS, D), BF16),
            pltpu.VMEM((D, HD), BF16),
            pltpu.VMEM((D, D), BF16),
            pltpu.VMEM((D, D), BF16),
            pltpu.VMEM((NP, 4 * COLS, ROWS * 128), BF16),
            pltpu.VMEM((NP, SITES, ROWS * 128), BF16),
            pltpu.VMEM((NP, SITES, ROWS * 128), BF16),
            pltpu.VMEM((8, NZ, PIECE, 128), F32),
            pltpu.VMEM((NP * 128, 128), F32),
            pltpu.VMEM((8, NZ, PIECE, 128), F32),
            pltpu.VMEM((8, PIECE, 128), F32),
            pltpu.VMEM((8, PIECE, 128), F32),
            pltpu.VMEM((NZ, 8, PIECE, 128), BF16),
            pltpu.VMEM((NZ, 1, 128), F32),
            pltpu.VMEM((NZ, OWNED, SITES + 128), BF16),
            pltpu.VMEM((2, NP, 2 * COLS, ROWS * 128), F32),
            pltpu.VMEM((NP, ROWS, COLS, 128), BF16),
            pltpu.VMEM((ROWS, COLS, D), BF16),
            pltpu.SemaphoreType.DMA((6,)),
            pltpu.SemaphoreType.DMA((4,)),
            pltpu.SemaphoreType.DMA((2,)),
            pltpu.SemaphoreType.DMA((8, 4)),
            pltpu.SemaphoreType.DMA((8, 2)),
            pltpu.SemaphoreType.DMA,
            pltpu.SemaphoreType.DMA((8,)),
            pltpu.SemaphoreType.DMA,
            pltpu.SemaphoreType.DMA((8,)),
            pltpu.SemaphoreType.DMA,
            pltpu.SemaphoreType.DMA((4,)),
            pltpu.SemaphoreType.DMA,
            pltpu.SemaphoreType.DMA,
            pltpu.SemaphoreType.DMA((NP,)),
            pltpu.SemaphoreType.DMA((NP,)),
        ],
        compiler_params=pltpu.CompilerParams(
            collective_id=0, has_side_effects=True, vmem_limit_bytes=58 * 2**20
        ),
        name="tied_rows",
    )(
        alignment_embedding,
        probe_projector,
        lookup_projector,
        content_projector,
        final_projector,
    )


def solution(mesh):
    placed = (P("seq", "res", None), P(), P(), P(), P())
    return jax.shard_map(
        body, mesh=mesh, in_specs=placed, out_specs=P("seq", "res", None), check_vma=False
    )
```

```python
import math

import jax
import jax.numpy as jnp
from jax import lax
from jax.experimental import pallas as pl
from jax.experimental.pallas import tpu as pltpu
from jax.sharding import PartitionSpec as P

MESH = pl.DeviceIdType.MESH
BF16, F32 = jnp.bfloat16, jnp.float32

H = 12
E = 64
D = 768
ROWS = 16
COLS = 32
NSEQ = 16
HD = D // 2
NP = HD // 128
SITES = 512

O, Y, L, R, YL, YR, OPP, YOPP = range(8)
PARTS = {b: ((0, 5), (5, 4), (9, 3), (12, 4)) for b in range(8)}
PARTS[YOPP] = ((0, 5), (5, 5), (10, 3), (13, 3))
UNIT = 2 * COLS
NZ = 8
OWNED = HD * UNIT // E // NZ
PIECE = OWNED // 2


def kernel(
    x_hbm,
    wq_hbm,
    wk_hbm,
    wv_hbm,
    wo_hbm,
    out_ref,
    xs,
    wq,
    wkv,
    wo,
    qp,
    kp,
    vp,
    ls,
    lbuf,
    rz,
    sz,
    ry,
    pall,
    factors,
    pfull,
    parts,
    half,
    full,
    in_sem,
    tx_sem,
    rx_sem,
    mate_sem,
    ltx_sem,
    lrx_sem,
    ytx_sem,
    yrx_sem,
    ptx_sem,
    prx_sem,
    ftx_sem,
    frx_sem,
    htx_sem,
    hrx_sem,
):
    s, r = lax.axis_index("seq"), lax.axis_index("res")
    z, yl = s // 2, lax.rem(s, 2)
    ix, yh, core = r // 4, lax.rem(r // 2, 2), lax.rem(r, 2)

    def at(dx, dy, dc):
        return (s, lax.rem(ix + dx + 4, 4) * 4 + lax.rem(yh + dy, 2) * 2 + lax.rem(core + dc, 2))

    right, left, across, mate = at(1, 0, 0), at(-1, 0, 0), at(0, 1, 0), at(0, 0, 1)

    def above(d):
        return (lax.rem(z + d, NZ) * 2 + yl, r)

    twin = (z * 2 + 1 - yl, r)

    barrier = pltpu.get_barrier_semaphore()
    for device in (right, left, across, mate, twin, *(above(d) for d in range(1, NZ))):
        pl.semaphore_signal(barrier, inc=1, device_id=device, device_id_type=MESH)

    mine = pl.ds(pl.multiple_of(core * HD, HD), HD)
    others = pl.ds(pl.multiple_of((1 - core) * HD, HD), HD)
    loads = [
        pltpu.make_async_copy(x_hbm, xs.at[O, 0], in_sem.at[0]),
        pltpu.make_async_copy(wq_hbm.at[:, mine], wq, in_sem.at[1]),
        pltpu.make_async_copy(wk_hbm.at[:, mine], wkv.at[:, pl.ds(0, HD)], in_sem.at[2]),
        pltpu.make_async_copy(wv_hbm.at[:, mine], wkv.at[:, pl.ds(HD, HD)], in_sem.at[3]),
        pltpu.make_async_copy(wo_hbm.at[mine, :], wo.at[pl.ds(0, HD)], in_sem.at[4]),
        pltpu.make_async_copy(wo_hbm.at[others, :], wo.at[pl.ds(HD, HD)], in_sem.at[5]),
    ]
    for copy in loads:
        copy.start()
    pl.semaphore_wait(barrier, 5 + NZ - 1)

    def send(block, part, device, landing):
        rows = pl.ds(*PARTS[landing][part])
        pltpu.make_async_remote_copy(
            src_ref=x_hbm.at[rows] if block == O else xs.at[block, 0, rows],
            dst_ref=xs.at[landing, 0, rows],
            send_sem=tx_sem.at[0],
            recv_sem=rx_sem.at[landing, part],
            device_id=device,
            device_id_type=MESH,
        ).start()

    def hand_on(block, part):
        rows = pl.ds(*PARTS[block][part])
        pltpu.make_async_remote_copy(
            src_ref=x_hbm.at[rows] if block == O else xs.at[block, 0, rows],
            dst_ref=xs.at[block, 1, rows],
            send_sem=tx_sem.at[1],
            recv_sem=mate_sem.at[block, part // 2],
            device_id=mate,
            device_id_type=MESH,
        ).start()

    def received(ref, recv_sem):
        return pltpu.make_async_remote_copy(
            src_ref=ref,
            dst_ref=ref,
            send_sem=tx_sem.at[0],
            recv_sem=recv_sem,
            device_id=mate,
            device_id_type=MESH,
        )

    def take(block, *parts):
        for part in parts:
            received(xs.at[block, 0, pl.ds(*PARTS[block][part])], rx_sem.at[block, part]).wait_recv()
            hand_on(block, part)

    def from_mate(block, *halves):
        for side in halves or (0, 1):
            (first, some), (_, more) = PARTS[block][2 * side : 2 * side + 2]
            ref = xs.at[block, 1, pl.ds(first, some + more)]
            received(ref, mate_sem.at[block, side]).wait_recv()

    def project_rows(block, cr, first, rows, pairs):
        x = xs[block, cr, pl.ds(first, rows)].reshape(rows * COLS, D)
        w = wkv[:, pl.ds(pairs[0] * 128, len(pairs) * 128)]
        y = jnp.dot(x, w, preferred_element_type=F32).astype(BF16)
        j = pl.ds(pl.multiple_of((2 * block + cr) * COLS, COLS), COLS)
        for row in range(rows):
            lanes = pl.ds((first + row) * 128, 128)
            for n, pair in enumerate(pairs):
                here = y[row * COLS : (row + 1) * COLS, n * 128 : (n + 1) * 128]
                if pair < NP:
                    kp[pair, j, lanes] = here
                else:
                    vp[pair - NP, j, lanes] = here

    def project_kv(block, pairs=range(2 * NP)):
        def one(cr, _):
            project_rows(block, cr, 0, ROWS, pairs)
            return 0

        lax.fori_loop(0, 2, one, 0)

    early, late = range(0, NP + 1), range(NP + 1, 2 * NP)

    def project_part(block, cr, side):
        (first, some), (_, more) = PARTS[block][2 * side : 2 * side + 2]
        project_rows(block, cr, first, some + more, early)

    def project_q(cr):
        x = xs[O, cr].reshape(ROWS * COLS, D)
        y = jnp.dot(x, wq[...], preferred_element_type=F32).astype(BF16)
        low = lax.broadcasted_iota(jnp.int32, (COLS, 128), 1) < E
        zero = jnp.zeros((COLS, 128), BF16)
        for row in range(ROWS):
            for pair in range(NP):
                q = y[row * COLS : (row + 1) * COLS, pair * 128 : (pair + 1) * 128]
                lanes = pl.ds(row * 128, 128)
                qp[pair, pl.ds(cr * COLS, COLS), lanes] = jnp.where(low, q, zero)
                qp[pair, pl.ds(2 * COLS + cr * COLS, COLS), lanes] = jnp.where(low, zero, q)

    low = lax.broadcasted_iota(jnp.int32, (PIECE, 128), 1) < UNIT

    def logits(unit):
        for pair in range(NP):
            k = kp[pair, pl.ds(unit * UNIT, UNIT), :]
            lbuf[pl.ds(pair * 128, 128), :] = lax.dot_general(
                qp[pair],
                jnp.concatenate([k, k], axis=0),
                (((1,), (1,)), ((), ())),
                preferred_element_type=F32,
            )
        for owner in range(NZ):
            ls[unit, owner] = jnp.where(
                low,
                lbuf[pl.ds(owner * OWNED, PIECE), :],
                lbuf[pl.ds(owner * OWNED + PIECE, PIECE), :],
            )

        def along_z(d, _):
            to = lax.rem(z + d, NZ)
            pltpu.make_async_remote_copy(
                src_ref=ls.at[unit, to],
                dst_ref=rz.at[unit, z],
                send_sem=ltx_sem,
                recv_sem=lrx_sem.at[unit],
                device_id=(to * 2 + yl, r),
                device_id_type=MESH,
            ).start()
            return 0

        lax.fori_loop(1, NZ, along_z, 0)
        rz[unit, z] = ls[unit, z]

    scale = 1.0 / math.sqrt(E * ROWS * NSEQ)

    def group(ref, send_sem, recv_sem):
        return pltpu.make_async_remote_copy(
            src_ref=ref,
            dst_ref=ref,
            send_sem=send_sem,
            recv_sem=recv_sem,
            device_id=mate,
            device_id_type=MESH,
        )

    def fold(unit):
        group(rz.at[unit, pl.ds(0, NZ - 1)], ltx_sem, lrx_sem.at[unit]).wait_recv()
        sz[unit] = jnp.sum(rz[unit], axis=0)
        pltpu.make_async_remote_copy(
            src_ref=sz.at[unit],
            dst_ref=ry.at[unit],
            send_sem=ytx_sem,
            recv_sem=yrx_sem.at[unit],
            device_id=twin,
            device_id_type=MESH,
        ).start()

    def halves(reduce, x, fill):
        first = reduce(jnp.where(low, x, fill), axis=1, keepdims=True)
        second = reduce(jnp.where(low, fill, x), axis=1, keepdims=True)
        return jnp.where(low, first, second)

    def scores_of(unit):
        group(ry.at[unit], ytx_sem, yrx_sem.at[unit]).wait_recv()
        return (sz[unit] + ry[unit]) * scale

    stats = []

    def absorb(*units):
        scores = [scores_of(unit) for unit in units]
        top = scores[0]
        for other in scores[1:]:
            top = jnp.maximum(top, other)
        top = halves(jnp.max, top, -jnp.inf)
        total = jnp.zeros((PIECE, 128), F32)
        for unit, score in zip(units, scores):
            weights = jnp.exp(score - top)
            total = total + weights
            pall[z, unit] = weights.astype(BF16)
        stats.append((top, halves(jnp.sum, total, 0.0)))

    def to_line(ref, send_sem, recv_sem):
        def one(d, _):
            pltpu.make_async_remote_copy(
                src_ref=ref,
                dst_ref=ref,
                send_sem=send_sem,
                recv_sem=recv_sem,
                device_id=above(d),
                device_id_type=MESH,
            ).start()
            return 0

        lax.fori_loop(1, NZ, one, 0)

    def spread(first, count, number):
        to_line(pall.at[z, pl.ds(first, count)], ptx_sem, prx_sem.at[number])

    def shared(first, count, number):
        ref = pall.at[pl.ds(0, NZ - 1), pl.ds(first, count)]
        group(ref, ptx_sem, prx_sem.at[number]).wait_recv()

    lane = lax.broadcasted_iota(jnp.int32, (PIECE, 128), 1)
    row_of = lax.broadcasted_iota(jnp.int32, (PIECE, 128), 0)

    def finish(unit):
        scores = scores_of(unit)
        top = halves(jnp.max, scores, -jnp.inf)
        for earlier, _ in stats:
            top = jnp.maximum(top, earlier)
        weights = jnp.exp(scores - top)
        total = halves(jnp.sum, weights, 0.0)
        scales = [jnp.exp(earlier - top) for earlier, _ in stats]
        for earlier, (_, part) in zip(scales, stats):
            total = total + earlier * part
        pall[z, unit] = (weights / total).astype(BF16)
        spread(unit, 1, 3)
        placed = jnp.zeros((PIECE, 128), F32)
        for number, earlier in enumerate(scales):
            here = lax.rem(lane, UNIT) == row_of + 32 * number
            placed = jnp.where(here, earlier / total, placed)
        factors[z] = jnp.sum(placed, axis=0, keepdims=True)
        to_line(factors.at[z], ftx_sem, frx_sem)

    def unpack(left_unit, right_unit, tile):
        even, odd = (
            pall[:, u].astype(F32).reshape(NZ * PIECE, 128) for u in (left_unit, right_unit)
        )
        wide = lax.broadcasted_iota(jnp.int32, (NZ * PIECE, 128), 1) < UNIT
        first = jnp.where(wide, even, pltpu.roll(odd, UNIT, 1))
        second = jnp.where(wide, pltpu.roll(even, UNIT, 1), odd)
        lanes = pl.ds(tile * 128, 128)
        for n, rows in enumerate((first, second)):
            pfull[:, pl.ds(n * PIECE, PIECE), lanes] = rows.astype(BF16).reshape(NZ, PIECE, 128)

    def factor(number):
        l = lax.broadcasted_iota(jnp.int32, (OWNED, 128), 1)
        i = lax.broadcasted_iota(jnp.int32, (OWNED, 128), 0)
        at_lane = jnp.where(i < PIECE, i, i - PIECE + UNIT) + 32 * number
        row = jnp.broadcast_to(factors[...], (NZ, OWNED, 128))
        return jnp.sum(jnp.where((l == at_lane)[None], row, 0.0), axis=2, keepdims=True)

    first_head = lax.broadcasted_iota(jnp.int32, (2 * COLS, 128), 1) < E

    def by_head(x):
        return jnp.where(first_head, x[: 2 * COLS], x[2 * COLS :])

    def product(pair, tile, first, count):
        probs = pfull[:, :, pl.ds(tile * 128, -(-count // 128) * 128)].reshape(NP * 128, -1)
        probs = probs[pair * 128 : (pair + 1) * 128, :count]
        return jnp.dot(probs, vp[pair, pl.ds(first, count), :], preferred_element_type=F32)

    def attend(number, tile, first, count):
        for pair in range(NP):
            whole = product(pair, tile, first, count)
            for row in range(ROWS):
                cut = slice(row * 128, (row + 1) * 128)
                parts[number, pair, :, cut] = by_head(whole[:, cut])

    for part in (2, 3, 0, 1):
        send(O, part, right, L)
    for part in (3, 2, 1, 0):
        send(O, part, left, R)
    for part in range(4):
        send(O, part, across, Y)
    for part in range(4):
        hand_on(O, part)

    for copy in loads[:4]:
        copy.wait()
    project_q(0)
    from_mate(O)
    project_q(1)
    project_kv(O)
    take(L, 2)
    send(L, 2, right, OPP)
    take(R, 3)
    send(R, 3, left, OPP)
    logits(O)
    take(L, 3)
    take(R, 2)
    for part in (2, 3):
        send(L, part, across, YL)
    take(Y, 0, 1)
    for part in (0, 1):
        send(Y, part, right, YL)
    for part in (1, 0):
        send(Y, part, left, YR)
    take(L, 0)
    send(L, 0, right, OPP)
    take(R, 1)
    send(R, 1, left, OPP)
    take(Y, 2)
    take(L, 1)
    take(R, 0)
    take(Y, 3)
    from_mate(L)
    project_kv(L)
    send(R, 2, across, YR)
    logits(L)
    from_mate(R)
    project_kv(R)
    logits(R)
    take(OPP, 2, 3)
    from_mate(Y)
    project_kv(Y)
    logits(Y)
    take(YL, 0)
    send(YL, 0, right, YOPP)
    take(YR, 1, 2)
    send(YR, 1, left, YOPP)
    take(YL, 2, 3)
    fold(O)
    fold(L)
    send(R, 3, across, YR)
    take(YL, 1)
    fold(R)
    take(YR, 0)
    fold(Y)
    for part in (2, 3):
        send(OPP, part, across, YOPP)
    from_mate(YL)
    project_kv(YL)
    logits(YL)
    take(YR, 3)
    take(OPP, 0, 1)
    absorb(O, Y, L, R)
    spread(O, 2, 0)
    from_mate(YR)
    project_kv(YR)
    logits(YR)
    from_mate(OPP)
    project_kv(OPP)
    logits(OPP)
    take(YOPP, 2, 3)
    project_part(YOPP, 0, 1)
    take(YOPP, 0, 1)
    project_part(YOPP, 0, 0)
    from_mate(YOPP, 1)
    project_part(YOPP, 1, 1)
    from_mate(YOPP, 0)
    project_part(YOPP, 1, 0)
    logits(YOPP)

    spread(L, 2, 1)
    fold(YL)
    fold(YR)
    project_kv(YOPP, late)
    shared(O, 2, 0)
    unpack(O, Y, 0)
    fold(OPP)
    absorb(YL, YR, OPP)
    spread(YL, 3, 2)
    fold(YOPP)
    shared(L, 2, 1)
    unpack(L, R, 1)
    attend(0, 0, O * UNIT, 4 * UNIT)
    finish(YOPP)
    shared(YL, 3, 2)
    unpack(YL, YR, 2)
    unpack(OPP, OPP, 3)
    attend(1, 2, YL * UNIT, 3 * UNIT)
    group(factors.at[pl.ds(0, NZ - 1)], ftx_sem, frx_sem).wait_recv()
    scaling = [factor(number).reshape(NP * 128, 1) for number in range(2)]
    shared(YOPP, 1, 3)
    unpack(YOPP, YOPP, 4)

    handed = []
    for pair in range(NP):
        lanes = pl.ds(pair * 128, 128)
        last = product(pair, 4, YOPP * UNIT, UNIT)
        ranks = [by_head(jnp.broadcast_to(f[pair * 128 : (pair + 1) * 128], (128, 128))) for f in scaling]
        for row in range(ROWS):
            cut = slice(row * 128, (row + 1) * 128)
            picked = by_head(last[:, cut])
            for number, rank in enumerate(ranks):
                picked = picked + rank * parts[number, pair, :, cut]
            picked = picked.astype(BF16)
            full[row, :, lanes] = picked[:COLS]
            half[pair, row] = picked[COLS:]
        copy = pltpu.make_async_remote_copy(
            src_ref=half.at[pair],
            dst_ref=full.at[:, :, pl.ds(HD + pair * 128, 128)],
            send_sem=htx_sem.at[pair],
            recv_sem=hrx_sem.at[pair],
            device_id=mate,
            device_id_type=MESH,
        )
        copy.start()
        handed.append(copy)
    for copy in loads[4:]:
        copy.wait()
    for copy in handed:
        copy.wait_recv()
    for quarter in range(4):
        rows = pl.ds(quarter * 4, 4)
        mixed = jnp.dot(full[rows].reshape(4 * COLS, D), wo[...], preferred_element_type=F32)
        out_ref[rows] = mixed.astype(BF16).reshape(4, COLS, D)

    for count, way in ((7, 0), (8, 1)):
        ref = xs.at[pl.ds(0, count), 0]
        pltpu.make_async_remote_copy(
            src_ref=ref,
            dst_ref=ref,
            send_sem=tx_sem.at[way],
            recv_sem=mate_sem.at[0, 0],
            device_id=mate,
            device_id_type=MESH,
        ).wait_send()
    group(rz.at[:, pl.ds(0, NZ - 1)], ltx_sem, lrx_sem.at[0]).wait_send()
    group(sz, ytx_sem, yrx_sem.at[0]).wait_send()
    group(pall.at[pl.ds(0, NZ - 1)], ptx_sem, prx_sem.at[0]).wait_send()
    group(factors.at[pl.ds(0, NZ - 1)], ftx_sem, frx_sem).wait_send()
    for copy in handed:
        copy.wait_send()


def body(alignment_embedding, probe_projector, lookup_projector, content_projector, final_projector):
    hbm = pl.BlockSpec(memory_space=pl.ANY)
    return pl.pallas_call(
        kernel,
        out_shape=jax.ShapeDtypeStruct((ROWS, COLS, D), BF16),
        in_specs=[hbm] * 5,
        out_specs=pl.BlockSpec(memory_space=pltpu.VMEM),
        scratch_shapes=[
            pltpu.VMEM((8, 2, ROWS, COLS, D), BF16),
            pltpu.VMEM((D, HD), BF16),
            pltpu.VMEM((D, D), BF16),
            pltpu.VMEM((D, D), BF16),
            pltpu.VMEM((NP, 4 * COLS, ROWS * 128), BF16),
            pltpu.VMEM((NP, SITES, ROWS * 128), BF16),
            pltpu.VMEM((NP, SITES, ROWS * 128), BF16),
            pltpu.VMEM((8, NZ, PIECE, 128), F32),
            pltpu.VMEM((NP * 128, 128), F32),
            pltpu.VMEM((8, NZ, PIECE, 128), F32),
            pltpu.VMEM((8, PIECE, 128), F32),
            pltpu.VMEM((8, PIECE, 128), F32),
            pltpu.VMEM((NZ, 8, PIECE, 128), BF16),
            pltpu.VMEM((NZ, 1, 128), F32),
            pltpu.VMEM((NZ, OWNED, SITES + 128), BF16),
            pltpu.VMEM((2, NP, 2 * COLS, ROWS * 128), F32),
            pltpu.VMEM((NP, ROWS, COLS, 128), BF16),
            pltpu.VMEM((ROWS, COLS, D), BF16),
            pltpu.SemaphoreType.DMA((6,)),
            pltpu.SemaphoreType.DMA((2,)),
            pltpu.SemaphoreType.DMA((8, 4)),
            pltpu.SemaphoreType.DMA((8, 2)),
            pltpu.SemaphoreType.DMA,
            pltpu.SemaphoreType.DMA((8,)),
            pltpu.SemaphoreType.DMA,
            pltpu.SemaphoreType.DMA((8,)),
            pltpu.SemaphoreType.DMA,
            pltpu.SemaphoreType.DMA((4,)),
            pltpu.SemaphoreType.DMA,
            pltpu.SemaphoreType.DMA,
            pltpu.SemaphoreType.DMA((NP,)),
            pltpu.SemaphoreType.DMA((NP,)),
        ],
        compiler_params=pltpu.CompilerParams(
            collective_id=0, has_side_effects=True, vmem_limit_bytes=53 * 2**20
        ),
        name="tied_rows",
    )(
        alignment_embedding,
        probe_projector,
        lookup_projector,
        content_projector,
        final_projector,
    )


def solution(mesh):
    placed = (P("seq", "res", None), P(), P(), P(), P())
    return jax.shard_map(
        body, mesh=mesh, in_specs=placed, out_specs=P("seq", "res", None), check_vma=False
    )
```

```python
import math

import jax
import jax.numpy as jnp
from jax import lax
from jax.experimental import pallas as pl
from jax.experimental.pallas import tpu as pltpu
from jax.sharding import PartitionSpec as P

MESH = pl.DeviceIdType.MESH
BF16, F32 = jnp.bfloat16, jnp.float32

H = 12
E = 64
D = 768
ROWS = 16
COLS = 32
NSEQ = 16
HD = D // 2
NP = HD // 128
SITES = 512

O, Y, L, R, YL, YR, OPP, YOPP = range(8)
PARTS = {b: ((0, 5), (5, 4), (9, 3), (12, 4)) for b in range(8)}
PARTS[YOPP] = ((0, 5), (5, 5), (10, 3), (13, 3))
UNIT = 2 * COLS
NZ = 8
OWNED = HD * UNIT // E // NZ
PIECE = OWNED // 2


def kernel(
    x_hbm,
    wq_hbm,
    wk_hbm,
    wv_hbm,
    wo_hbm,
    out_ref,
    xs,
    wq,
    wkv,
    wo,
    qp,
    kp,
    vp,
    ls,
    lbuf,
    rz,
    sz,
    ry,
    pall,
    factors,
    pfull,
    parts,
    half,
    full,
    in_sem,
    tx_sem,
    rx_sem,
    mate_sem,
    ltx_sem,
    lrx_sem,
    ytx_sem,
    yrx_sem,
    ptx_sem,
    prx_sem,
    ftx_sem,
    frx_sem,
    htx_sem,
    hrx_sem,
):
    s, r = lax.axis_index("seq"), lax.axis_index("res")
    z, yl = s // 2, lax.rem(s, 2)
    ix, yh, core = r // 4, lax.rem(r // 2, 2), lax.rem(r, 2)

    def at(dx, dy, dc):
        return (s, lax.rem(ix + dx + 4, 4) * 4 + lax.rem(yh + dy, 2) * 2 + lax.rem(core + dc, 2))

    right, left, across, mate = at(1, 0, 0), at(-1, 0, 0), at(0, 1, 0), at(0, 0, 1)

    def far_first(k):
        return 4 + (k + 1) // 2 * (1 - 2 * lax.rem(k, 2))

    def above(d):
        return (lax.rem(z + d, NZ) * 2 + yl, r)

    twin = (z * 2 + 1 - yl, r)

    barrier = pltpu.get_barrier_semaphore()
    for device in (right, left, across, mate, twin, *(above(d) for d in range(1, NZ))):
        pl.semaphore_signal(barrier, inc=1, device_id=device, device_id_type=MESH)

    mine = pl.ds(pl.multiple_of(core * HD, HD), HD)
    others = pl.ds(pl.multiple_of((1 - core) * HD, HD), HD)
    loads = [
        pltpu.make_async_copy(x_hbm, xs.at[O, 0], in_sem.at[0]),
        pltpu.make_async_copy(wq_hbm.at[:, mine], wq, in_sem.at[1]),
        pltpu.make_async_copy(wk_hbm.at[:, mine], wkv.at[:, pl.ds(0, HD)], in_sem.at[2]),
        pltpu.make_async_copy(wv_hbm.at[:, mine], wkv.at[:, pl.ds(HD, HD)], in_sem.at[3]),
        pltpu.make_async_copy(wo_hbm.at[mine, :], wo.at[pl.ds(0, HD)], in_sem.at[4]),
        pltpu.make_async_copy(wo_hbm.at[others, :], wo.at[pl.ds(HD, HD)], in_sem.at[5]),
    ]
    for copy in loads:
        copy.start()
    pl.semaphore_wait(barrier, 5 + NZ - 1)

    def send(block, part, device, landing):
        rows = pl.ds(*PARTS[landing][part])
        pltpu.make_async_remote_copy(
            src_ref=x_hbm.at[rows] if block == O else xs.at[block, 0, rows],
            dst_ref=xs.at[landing, 0, rows],
            send_sem=tx_sem.at[0],
            recv_sem=rx_sem.at[landing, part],
            device_id=device,
            device_id_type=MESH,
        ).start()

    def hand_on(block, part):
        rows = pl.ds(*PARTS[block][part])
        pltpu.make_async_remote_copy(
            src_ref=x_hbm.at[rows] if block == O else xs.at[block, 0, rows],
            dst_ref=xs.at[block, 1, rows],
            send_sem=tx_sem.at[1],
            recv_sem=mate_sem.at[block, part // 2],
            device_id=mate,
            device_id_type=MESH,
        ).start()

    def received(ref, recv_sem):
        return pltpu.make_async_remote_copy(
            src_ref=ref,
            dst_ref=ref,
            send_sem=tx_sem.at[0],
            recv_sem=recv_sem,
            device_id=mate,
            device_id_type=MESH,
        )

    def take(block, *parts):
        for part in parts:
            received(xs.at[block, 0, pl.ds(*PARTS[block][part])], rx_sem.at[block, part]).wait_recv()
            hand_on(block, part)

    def from_mate(block, *halves):
        for side in halves or (0, 1):
            (first, some), (_, more) = PARTS[block][2 * side : 2 * side + 2]
            ref = xs.at[block, 1, pl.ds(first, some + more)]
            received(ref, mate_sem.at[block, side]).wait_recv()

    def project_rows(block, cr, first, rows, pairs):
        x = xs[block, cr, pl.ds(first, rows)].reshape(rows * COLS, D)
        w = wkv[:, pl.ds(pairs[0] * 128, len(pairs) * 128)]
        y = jnp.dot(x, w, preferred_element_type=F32).astype(BF16)
        j = pl.ds(pl.multiple_of((2 * block + cr) * COLS, COLS), COLS)
        for row in range(rows):
            lanes = pl.ds((first + row) * 128, 128)
            for n, pair in enumerate(pairs):
                here = y[row * COLS : (row + 1) * COLS, n * 128 : (n + 1) * 128]
                if pair < NP:
                    kp[pair, j, lanes] = here
                else:
                    vp[pair - NP, j, lanes] = here

    def project_kv(block, pairs=range(2 * NP)):
        def one(cr, _):
            project_rows(block, cr, 0, ROWS, pairs)
            return 0

        lax.fori_loop(0, 2, one, 0)

    early, late = range(0, NP + 1), range(NP + 1, 2 * NP)

    def project_part(block, cr, side):
        (first, some), (_, more) = PARTS[block][2 * side : 2 * side + 2]
        project_rows(block, cr, first, some + more, early)

    def project_q(cr):
        x = xs[O, cr].reshape(ROWS * COLS, D)
        y = jnp.dot(x, wq[...], preferred_element_type=F32).astype(BF16)
        low = lax.broadcasted_iota(jnp.int32, (COLS, 128), 1) < E
        zero = jnp.zeros((COLS, 128), BF16)
        for row in range(ROWS):
            for pair in range(NP):
                q = y[row * COLS : (row + 1) * COLS, pair * 128 : (pair + 1) * 128]
                lanes = pl.ds(row * 128, 128)
                qp[pair, pl.ds(cr * COLS, COLS), lanes] = jnp.where(low, q, zero)
                qp[pair, pl.ds(2 * COLS + cr * COLS, COLS), lanes] = jnp.where(low, zero, q)

    low = lax.broadcasted_iota(jnp.int32, (PIECE, 128), 1) < UNIT

    def logits(unit):
        for pair in range(NP):
            k = kp[pair, pl.ds(unit * UNIT, UNIT), :]
            lbuf[pl.ds(pair * 128, 128), :] = lax.dot_general(
                qp[pair],
                jnp.concatenate([k, k], axis=0),
                (((1,), (1,)), ((), ())),
                preferred_element_type=F32,
            )
        for owner in range(NZ):
            ls[unit, owner] = jnp.where(
                low,
                lbuf[pl.ds(owner * OWNED, PIECE), :],
                lbuf[pl.ds(owner * OWNED + PIECE, PIECE), :],
            )

        def along_z(k, _):
            to = lax.rem(z + far_first(k), NZ)
            pltpu.make_async_remote_copy(
                src_ref=ls.at[unit, to],
                dst_ref=rz.at[unit, z],
                send_sem=ltx_sem,
                recv_sem=lrx_sem.at[unit],
                device_id=(to * 2 + yl, r),
                device_id_type=MESH,
            ).start()
            return 0

        lax.fori_loop(0, NZ - 1, along_z, 0)
        rz[unit, z] = ls[unit, z]

    scale = 1.0 / math.sqrt(E * ROWS * NSEQ)

    def group(ref, send_sem, recv_sem):
        return pltpu.make_async_remote_copy(
            src_ref=ref,
            dst_ref=ref,
            send_sem=send_sem,
            recv_sem=recv_sem,
            device_id=mate,
            device_id_type=MESH,
        )

    def fold(unit):
        group(rz.at[unit, pl.ds(0, NZ - 1)], ltx_sem, lrx_sem.at[unit]).wait_recv()
        sz[unit] = jnp.sum(rz[unit], axis=0)
        pltpu.make_async_remote_copy(
            src_ref=sz.at[unit],
            dst_ref=ry.at[unit],
            send_sem=ytx_sem,
            recv_sem=yrx_sem.at[unit],
            device_id=twin,
            device_id_type=MESH,
        ).start()

    def halves(reduce, x, fill):
        first = reduce(jnp.where(low, x, fill), axis=1, keepdims=True)
        second = reduce(jnp.where(low, fill, x), axis=1, keepdims=True)
        return jnp.where(low, first, second)

    def scores_of(unit):
        group(ry.at[unit], ytx_sem, yrx_sem.at[unit]).wait_recv()
        return (sz[unit] + ry[unit]) * scale

    stats = []

    def absorb(*units):
        scores = [scores_of(unit) for unit in units]
        top = scores[0]
        for other in scores[1:]:
            top = jnp.maximum(top, other)
        top = halves(jnp.max, top, -jnp.inf)
        total = jnp.zeros((PIECE, 128), F32)
        for unit, score in zip(units, scores):
            weights = jnp.exp(score - top)
            total = total + weights
            pall[z, unit] = weights.astype(BF16)
        stats.append((top, halves(jnp.sum, total, 0.0)))

    def to_line(ref, send_sem, recv_sem):
        def one(k, _):
            pltpu.make_async_remote_copy(
                src_ref=ref,
                dst_ref=ref,
                send_sem=send_sem,
                recv_sem=recv_sem,
                device_id=above(far_first(k)),
                device_id_type=MESH,
            ).start()
            return 0

        lax.fori_loop(0, NZ - 1, one, 0)

    def spread(first, count, number):
        to_line(pall.at[z, pl.ds(first, count)], ptx_sem, prx_sem.at[number])

    def shared(first, count, number):
        ref = pall.at[pl.ds(0, NZ - 1), pl.ds(first, count)]
        group(ref, ptx_sem, prx_sem.at[number]).wait_recv()

    lane = lax.broadcasted_iota(jnp.int32, (PIECE, 128), 1)
    row_of = lax.broadcasted_iota(jnp.int32, (PIECE, 128), 0)

    def finish(unit):
        scores = scores_of(unit)
        top = halves(jnp.max, scores, -jnp.inf)
        for earlier, _ in stats:
            top = jnp.maximum(top, earlier)
        weights = jnp.exp(scores - top)
        total = halves(jnp.sum, weights, 0.0)
        scales = [jnp.exp(earlier - top) for earlier, _ in stats]
        for earlier, (_, part) in zip(scales, stats):
            total = total + earlier * part
        pall[z, unit] = (weights / total).astype(BF16)
        spread(unit, 1, 3)
        placed = jnp.zeros((PIECE, 128), F32)
        for number, earlier in enumerate(scales):
            here = lax.rem(lane, UNIT) == row_of + 32 * number
            placed = jnp.where(here, earlier / total, placed)
        factors[z] = jnp.sum(placed, axis=0, keepdims=True)
        to_line(factors.at[z], ftx_sem, frx_sem)

    def unpack(left_unit, right_unit, tile):
        even, odd = (
            pall[:, u].astype(F32).reshape(NZ * PIECE, 128) for u in (left_unit, right_unit)
        )
        wide = lax.broadcasted_iota(jnp.int32, (NZ * PIECE, 128), 1) < UNIT
        first = jnp.where(wide, even, pltpu.roll(odd, UNIT, 1))
        second = jnp.where(wide, pltpu.roll(even, UNIT, 1), odd)
        lanes = pl.ds(tile * 128, 128)
        for n, rows in enumerate((first, second)):
            pfull[:, pl.ds(n * PIECE, PIECE), lanes] = rows.astype(BF16).reshape(NZ, PIECE, 128)

    def factor(number):
        l = lax.broadcasted_iota(jnp.int32, (OWNED, 128), 1)
        i = lax.broadcasted_iota(jnp.int32, (OWNED, 128), 0)
        at_lane = jnp.where(i < PIECE, i, i - PIECE + UNIT) + 32 * number
        row = jnp.broadcast_to(factors[...], (NZ, OWNED, 128))
        return jnp.sum(jnp.where((l == at_lane)[None], row, 0.0), axis=2, keepdims=True)

    first_head = lax.broadcasted_iota(jnp.int32, (2 * COLS, 128), 1) < E

    def by_head(x):
        return jnp.where(first_head, x[: 2 * COLS], x[2 * COLS :])

    def product(pair, tile, first, count):
        probs = pfull[:, :, pl.ds(tile * 128, -(-count // 128) * 128)].reshape(NP * 128, -1)
        probs = probs[pair * 128 : (pair + 1) * 128, :count]
        return jnp.dot(probs, vp[pair, pl.ds(first, count), :], preferred_element_type=F32)

    def attend(number, tile, first, count):
        for pair in range(NP):
            whole = product(pair, tile, first, count)
            for row in range(ROWS):
                cut = slice(row * 128, (row + 1) * 128)
                parts[number, pair, :, cut] = by_head(whole[:, cut])

    for part in (2, 3, 0, 1):
        send(O, part, right, L)
    for part in (3, 2, 1, 0):
        send(O, part, left, R)
    for part in range(4):
        send(O, part, across, Y)
    for part in range(4):
        hand_on(O, part)

    for copy in loads[:4]:
        copy.wait()
    project_q(0)
    from_mate(O)
    project_q(1)
    project_kv(O)
    take(L, 2)
    send(L, 2, right, OPP)
    take(R, 3)
    send(R, 3, left, OPP)
    logits(O)
    take(L, 3)
    take(R, 2)
    for part in (2, 3):
        send(L, part, across, YL)
    take(Y, 0, 1)
    for part in (0, 1):
        send(Y, part, right, YL)
    for part in (1, 0):
        send(Y, part, left, YR)
    take(L, 0)
    send(L, 0, right, OPP)
    take(R, 1)
    send(R, 1, left, OPP)
    take(Y, 2)
    take(L, 1)
    take(R, 0)
    take(Y, 3)
    from_mate(L)
    project_kv(L)
    send(R, 2, across, YR)
    logits(L)
    from_mate(R)
    project_kv(R)
    logits(R)
    take(OPP, 2, 3)
    from_mate(Y)
    project_kv(Y)
    logits(Y)
    take(YL, 0)
    send(YL, 0, right, YOPP)
    take(YR, 1, 2)
    send(YR, 1, left, YOPP)
    take(YL, 2, 3)
    fold(O)
    fold(L)
    send(R, 3, across, YR)
    take(YL, 1)
    fold(R)
    take(YR, 0)
    fold(Y)
    for part in (2, 3):
        send(OPP, part, across, YOPP)
    from_mate(YL)
    project_kv(YL)
    logits(YL)
    take(YR, 3)
    take(OPP, 0, 1)
    absorb(O, Y, L, R)
    spread(O, 2, 0)
    from_mate(YR)
    project_kv(YR)
    logits(YR)
    from_mate(OPP)
    project_kv(OPP)
    logits(OPP)
    take(YOPP, 2, 3)
    take(YOPP, 0, 1)
    project_part(YOPP, 0, 1)
    project_part(YOPP, 0, 0)
    from_mate(YOPP, 1)
    project_part(YOPP, 1, 1)
    from_mate(YOPP, 0)
    project_part(YOPP, 1, 0)
    logits(YOPP)

    spread(L, 2, 1)
    fold(YL)
    fold(YR)
    project_kv(YOPP, late)
    shared(O, 2, 0)
    unpack(O, Y, 0)
    fold(OPP)
    absorb(YL, YR, OPP)
    spread(YL, 3, 2)
    fold(YOPP)
    shared(L, 2, 1)
    unpack(L, R, 1)
    attend(0, 0, O * UNIT, 4 * UNIT)
    finish(YOPP)
    shared(YL, 3, 2)
    unpack(YL, YR, 2)
    unpack(OPP, OPP, 3)
    attend(1, 2, YL * UNIT, 3 * UNIT)
    group(factors.at[pl.ds(0, NZ - 1)], ftx_sem, frx_sem).wait_recv()
    scaling = [factor(number).reshape(NP * 128, 1) for number in range(2)]
    shared(YOPP, 1, 3)
    unpack(YOPP, YOPP, 4)

    handed = []
    for pair in range(NP):
        lanes = pl.ds(pair * 128, 128)
        last = product(pair, 4, YOPP * UNIT, UNIT)
        ranks = [by_head(jnp.broadcast_to(f[pair * 128 : (pair + 1) * 128], (128, 128))) for f in scaling]
        for row in range(ROWS):
            cut = slice(row * 128, (row + 1) * 128)
            picked = by_head(last[:, cut])
            for number, rank in enumerate(ranks):
                picked = picked + rank * parts[number, pair, :, cut]
            picked = picked.astype(BF16)
            full[row, :, lanes] = picked[:COLS]
            half[pair, row] = picked[COLS:]
        copy = pltpu.make_async_remote_copy(
            src_ref=half.at[pair],
            dst_ref=full.at[:, :, pl.ds(HD + pair * 128, 128)],
            send_sem=htx_sem.at[pair],
            recv_sem=hrx_sem.at[pair],
            device_id=mate,
            device_id_type=MESH,
        )
        copy.start()
        handed.append(copy)
    for copy in loads[4:]:
        copy.wait()
    for copy in handed:
        copy.wait_recv()
    mixed = jnp.dot(full[...].reshape(ROWS * COLS, D), wo[...], preferred_element_type=F32)
    out_ref[...] = mixed.astype(BF16).reshape(ROWS, COLS, D)

    for count, way in ((7, 0), (8, 1)):
        ref = xs.at[pl.ds(0, count), 0]
        pltpu.make_async_remote_copy(
            src_ref=ref,
            dst_ref=ref,
            send_sem=tx_sem.at[way],
            recv_sem=mate_sem.at[0, 0],
            device_id=mate,
            device_id_type=MESH,
        ).wait_send()
    group(rz.at[:, pl.ds(0, NZ - 1)], ltx_sem, lrx_sem.at[0]).wait_send()
    group(sz, ytx_sem, yrx_sem.at[0]).wait_send()
    group(pall.at[pl.ds(0, NZ - 1)], ptx_sem, prx_sem.at[0]).wait_send()
    group(factors.at[pl.ds(0, NZ - 1)], ftx_sem, frx_sem).wait_send()
    for copy in handed:
        copy.wait_send()


def body(alignment_embedding, probe_projector, lookup_projector, content_projector, final_projector):
    hbm = pl.BlockSpec(memory_space=pl.ANY)
    return pl.pallas_call(
        kernel,
        out_shape=jax.ShapeDtypeStruct((ROWS, COLS, D), BF16),
        in_specs=[hbm] * 5,
        out_specs=pl.BlockSpec(memory_space=pltpu.VMEM),
        scratch_shapes=[
            pltpu.VMEM((8, 2, ROWS, COLS, D), BF16),
            pltpu.VMEM((D, HD), BF16),
            pltpu.VMEM((D, D), BF16),
            pltpu.VMEM((D, D), BF16),
            pltpu.VMEM((NP, 4 * COLS, ROWS * 128), BF16),
            pltpu.VMEM((NP, SITES, ROWS * 128), BF16),
            pltpu.VMEM((NP, SITES, ROWS * 128), BF16),
            pltpu.VMEM((8, NZ, PIECE, 128), F32),
            pltpu.VMEM((NP * 128, 128), F32),
            pltpu.VMEM((8, NZ, PIECE, 128), F32),
            pltpu.VMEM((8, PIECE, 128), F32),
            pltpu.VMEM((8, PIECE, 128), F32),
            pltpu.VMEM((NZ, 8, PIECE, 128), BF16),
            pltpu.VMEM((NZ, 1, 128), F32),
            pltpu.VMEM((NZ, OWNED, SITES + 128), BF16),
            pltpu.VMEM((2, NP, 2 * COLS, ROWS * 128), F32),
            pltpu.VMEM((NP, ROWS, COLS, 128), BF16),
            pltpu.VMEM((ROWS, COLS, D), BF16),
            pltpu.SemaphoreType.DMA((6,)),
            pltpu.SemaphoreType.DMA((2,)),
            pltpu.SemaphoreType.DMA((8, 4)),
            pltpu.SemaphoreType.DMA((8, 2)),
            pltpu.SemaphoreType.DMA,
            pltpu.SemaphoreType.DMA((8,)),
            pltpu.SemaphoreType.DMA,
            pltpu.SemaphoreType.DMA((8,)),
            pltpu.SemaphoreType.DMA,
            pltpu.SemaphoreType.DMA((4,)),
            pltpu.SemaphoreType.DMA,
            pltpu.SemaphoreType.DMA,
            pltpu.SemaphoreType.DMA((NP,)),
            pltpu.SemaphoreType.DMA((NP,)),
        ],
        compiler_params=pltpu.CompilerParams(
            collective_id=0, has_side_effects=True, vmem_limit_bytes=53 * 2**20
        ),
        name="tied_rows",
    )(
        alignment_embedding,
        probe_projector,
        lookup_projector,
        content_projector,
        final_projector,
    )


def solution(mesh):
    placed = (P("seq", "res", None), P(), P(), P(), P())
    return jax.shard_map(
        body, mesh=mesh, in_specs=placed, out_specs=P("seq", "res", None), check_vma=False
    )
```

```python
import math

import jax
import jax.numpy as jnp
from jax import lax
from jax.experimental import pallas as pl
from jax.experimental.pallas import tpu as pltpu
from jax.sharding import PartitionSpec as P

MESH = pl.DeviceIdType.MESH
BF16, F32 = jnp.bfloat16, jnp.float32

H = 12
E = 64
D = 768
ROWS = 16
COLS = 32
NSEQ = 16
HD = D // 2
NP = HD // 128
SITES = 512

O, Y, L, R, YL, YR, OPP, YOPP = range(8)
PARTS = {b: ((0, 5), (5, 4), (9, 3), (12, 4)) for b in range(8)}
PARTS[YOPP] = ((0, 5), (5, 5), (10, 3), (13, 3))
UNIT = 2 * COLS
NZ = 8
OWNED = HD * UNIT // E // NZ
PIECE = OWNED // 2


def kernel(
    x_hbm,
    wq_hbm,
    wk_hbm,
    wv_hbm,
    wo_hbm,
    out_ref,
    xs,
    wq,
    wkv,
    wo,
    qp,
    kp,
    vp,
    ls,
    lbuf,
    rz,
    sz,
    ry,
    pall,
    factors,
    pfull,
    parts,
    half,
    full,
    in_sem,
    tx_sem,
    rx_sem,
    mate_sem,
    ltx_sem,
    lrx_sem,
    ytx_sem,
    yrx_sem,
    ptx_sem,
    prx_sem,
    ftx_sem,
    frx_sem,
    htx_sem,
    hrx_sem,
):
    s, r = lax.axis_index("seq"), lax.axis_index("res")
    z, yl = s // 2, lax.rem(s, 2)
    ix, yh, core = r // 4, lax.rem(r // 2, 2), lax.rem(r, 2)

    def at(dx, dy, dc):
        return (s, lax.rem(ix + dx + 4, 4) * 4 + lax.rem(yh + dy, 2) * 2 + lax.rem(core + dc, 2))

    right, left, across, mate = at(1, 0, 0), at(-1, 0, 0), at(0, 1, 0), at(0, 0, 1)

    def far_first(k):
        return 4 + (k + 1) // 2 * (1 - 2 * lax.rem(k, 2))

    def above(d):
        return (lax.rem(z + d, NZ) * 2 + yl, r)

    twin = (z * 2 + 1 - yl, r)

    barrier = pltpu.get_barrier_semaphore()
    for device in (right, left, across, mate, twin, *(above(d) for d in range(1, NZ))):
        pl.semaphore_signal(barrier, inc=1, device_id=device, device_id_type=MESH)

    mine = pl.ds(pl.multiple_of(core * HD, HD), HD)
    others = pl.ds(pl.multiple_of((1 - core) * HD, HD), HD)
    loads = [
        pltpu.make_async_copy(x_hbm, xs.at[O, 0], in_sem.at[0]),
        pltpu.make_async_copy(wq_hbm.at[:, mine], wq, in_sem.at[1]),
        pltpu.make_async_copy(wk_hbm.at[:, mine], wkv.at[:, pl.ds(0, HD)], in_sem.at[2]),
        pltpu.make_async_copy(wv_hbm.at[:, mine], wkv.at[:, pl.ds(HD, HD)], in_sem.at[3]),
        pltpu.make_async_copy(wo_hbm.at[mine, :], wo.at[pl.ds(0, HD)], in_sem.at[4]),
        pltpu.make_async_copy(wo_hbm.at[others, :], wo.at[pl.ds(HD, HD)], in_sem.at[5]),
    ]
    for copy in loads:
        copy.start()
    pl.semaphore_wait(barrier, 5 + NZ - 1)

    def send(block, part, device, landing):
        rows = pl.ds(*PARTS[landing][part])
        pltpu.make_async_remote_copy(
            src_ref=x_hbm.at[rows] if block == O else xs.at[block, 0, rows],
            dst_ref=xs.at[landing, 0, rows],
            send_sem=tx_sem.at[0],
            recv_sem=rx_sem.at[landing, part],
            device_id=device,
            device_id_type=MESH,
        ).start()

    def hand_on(block, part):
        rows = pl.ds(*PARTS[block][part])
        pltpu.make_async_remote_copy(
            src_ref=x_hbm.at[rows] if block == O else xs.at[block, 0, rows],
            dst_ref=xs.at[block, 1, rows],
            send_sem=tx_sem.at[1],
            recv_sem=mate_sem.at[block, part // 2],
            device_id=mate,
            device_id_type=MESH,
        ).start()

    def received(ref, recv_sem):
        return pltpu.make_async_remote_copy(
            src_ref=ref,
            dst_ref=ref,
            send_sem=tx_sem.at[0],
            recv_sem=recv_sem,
            device_id=mate,
            device_id_type=MESH,
        )

    def take(block, *parts):
        for part in parts:
            received(xs.at[block, 0, pl.ds(*PARTS[block][part])], rx_sem.at[block, part]).wait_recv()
            hand_on(block, part)

    def from_mate(block, *halves):
        for side in halves or (0, 1):
            (first, some), (_, more) = PARTS[block][2 * side : 2 * side + 2]
            ref = xs.at[block, 1, pl.ds(first, some + more)]
            received(ref, mate_sem.at[block, side]).wait_recv()

    def project_rows(block, cr, first, rows, pairs):
        x = xs[block, cr, pl.ds(first, rows)].reshape(rows * COLS, D)
        w = wkv[:, pl.ds(pairs[0] * 128, len(pairs) * 128)]
        y = jnp.dot(x, w, preferred_element_type=F32).astype(BF16)
        j = pl.ds(pl.multiple_of((2 * block + cr) * COLS, COLS), COLS)
        for row in range(rows):
            lanes = pl.ds((first + row) * 128, 128)
            for n, pair in enumerate(pairs):
                here = y[row * COLS : (row + 1) * COLS, n * 128 : (n + 1) * 128]
                if pair < NP:
                    kp[pair, j, lanes] = here
                else:
                    vp[pair - NP, j, lanes] = here

    def project_kv(block, pairs=range(2 * NP)):
        def one(cr, _):
            project_rows(block, cr, 0, ROWS, pairs)
            return 0

        lax.fori_loop(0, 2, one, 0)

    early, late = range(0, NP + 1), range(NP + 1, 2 * NP)

    def project_part(block, cr, side):
        (first, some), (_, more) = PARTS[block][2 * side : 2 * side + 2]
        project_rows(block, cr, first, some + more, early)

    def project_q(cr):
        x = xs[O, cr].reshape(ROWS * COLS, D)
        y = jnp.dot(x, wq[...], preferred_element_type=F32).astype(BF16)
        low = lax.broadcasted_iota(jnp.int32, (COLS, 128), 1) < E
        zero = jnp.zeros((COLS, 128), BF16)
        for row in range(ROWS):
            for pair in range(NP):
                q = y[row * COLS : (row + 1) * COLS, pair * 128 : (pair + 1) * 128]
                lanes = pl.ds(row * 128, 128)
                qp[pair, pl.ds(cr * COLS, COLS), lanes] = jnp.where(low, q, zero)
                qp[pair, pl.ds(2 * COLS + cr * COLS, COLS), lanes] = jnp.where(low, zero, q)

    low = lax.broadcasted_iota(jnp.int32, (PIECE, 128), 1) < UNIT

    def logits(unit):
        for pair in range(NP):
            k = kp[pair, pl.ds(unit * UNIT, UNIT), :]
            lbuf[pl.ds(pair * 128, 128), :] = lax.dot_general(
                qp[pair],
                jnp.concatenate([k, k], axis=0),
                (((1,), (1,)), ((), ())),
                preferred_element_type=F32,
            )
        for owner in range(NZ):
            ls[unit, owner] = jnp.where(
                low,
                lbuf[pl.ds(owner * OWNED, PIECE), :],
                lbuf[pl.ds(owner * OWNED + PIECE, PIECE), :],
            )

        def along_z(k, _):
            to = lax.rem(z + far_first(k), NZ)
            pltpu.make_async_remote_copy(
                src_ref=ls.at[unit, to],
                dst_ref=rz.at[unit, z],
                send_sem=ltx_sem,
                recv_sem=lrx_sem.at[unit],
                device_id=(to * 2 + yl, r),
                device_id_type=MESH,
            ).start()
            return 0

        lax.fori_loop(0, NZ - 1, along_z, 0)
        rz[unit, z] = ls[unit, z]

    scale = 1.0 / math.sqrt(E * ROWS * NSEQ)

    def group(ref, send_sem, recv_sem):
        return pltpu.make_async_remote_copy(
            src_ref=ref,
            dst_ref=ref,
            send_sem=send_sem,
            recv_sem=recv_sem,
            device_id=mate,
            device_id_type=MESH,
        )

    def fold(unit):
        group(rz.at[unit, pl.ds(0, NZ - 1)], ltx_sem, lrx_sem.at[unit]).wait_recv()
        sz[unit] = jnp.sum(rz[unit], axis=0)
        pltpu.make_async_remote_copy(
            src_ref=sz.at[unit],
            dst_ref=ry.at[unit],
            send_sem=ytx_sem,
            recv_sem=yrx_sem.at[unit],
            device_id=twin,
            device_id_type=MESH,
        ).start()

    def halves(reduce, x, fill):
        first = reduce(jnp.where(low, x, fill), axis=1, keepdims=True)
        second = reduce(jnp.where(low, fill, x), axis=1, keepdims=True)
        return jnp.where(low, first, second)

    def scores_of(unit):
        group(ry.at[unit], ytx_sem, yrx_sem.at[unit]).wait_recv()
        return (sz[unit] + ry[unit]) * scale

    stats = []

    def absorb(*units):
        scores = [scores_of(unit) for unit in units]
        top = scores[0]
        for other in scores[1:]:
            top = jnp.maximum(top, other)
        top = halves(jnp.max, top, -jnp.inf)
        total = jnp.zeros((PIECE, 128), F32)
        for unit, score in zip(units, scores):
            weights = jnp.exp(score - top)
            total = total + weights
            pall[z, unit] = weights.astype(BF16)
        stats.append((top, halves(jnp.sum, total, 0.0)))

    def to_line(ref, send_sem, recv_sem):
        def one(k, _):
            pltpu.make_async_remote_copy(
                src_ref=ref,
                dst_ref=ref,
                send_sem=send_sem,
                recv_sem=recv_sem,
                device_id=above(far_first(k)),
                device_id_type=MESH,
            ).start()
            return 0

        lax.fori_loop(0, NZ - 1, one, 0)

    def spread(first, count, number):
        to_line(pall.at[z, pl.ds(first, count)], ptx_sem, prx_sem.at[number])

    def shared(first, count, number):
        ref = pall.at[pl.ds(0, NZ - 1), pl.ds(first, count)]
        group(ref, ptx_sem, prx_sem.at[number]).wait_recv()

    lane = lax.broadcasted_iota(jnp.int32, (PIECE, 128), 1)
    row_of = lax.broadcasted_iota(jnp.int32, (PIECE, 128), 0)

    def finish(unit):
        scores = scores_of(unit)
        top = halves(jnp.max, scores, -jnp.inf)
        for earlier, _ in stats:
            top = jnp.maximum(top, earlier)
        weights = jnp.exp(scores - top)
        total = halves(jnp.sum, weights, 0.0)
        scales = [jnp.exp(earlier - top) for earlier, _ in stats]
        for earlier, (_, part) in zip(scales, stats):
            total = total + earlier * part
        pall[z, unit] = (weights / total).astype(BF16)
        spread(unit, 1, 3)
        placed = jnp.zeros((PIECE, 128), F32)
        for number, earlier in enumerate(scales):
            here = lax.rem(lane, UNIT) == row_of + 32 * number
            placed = jnp.where(here, earlier / total, placed)
        factors[z] = jnp.sum(placed, axis=0, keepdims=True)
        to_line(factors.at[z], ftx_sem, frx_sem)

    def unpack(left_unit, right_unit, tile):
        even, odd = (
            pall[:, u].astype(F32).reshape(NZ * PIECE, 128) for u in (left_unit, right_unit)
        )
        wide = lax.broadcasted_iota(jnp.int32, (NZ * PIECE, 128), 1) < UNIT
        first = jnp.where(wide, even, pltpu.roll(odd, UNIT, 1))
        second = jnp.where(wide, pltpu.roll(even, UNIT, 1), odd)
        lanes = pl.ds(tile * 128, 128)
        for n, rows in enumerate((first, second)):
            pfull[:, pl.ds(n * PIECE, PIECE), lanes] = rows.astype(BF16).reshape(NZ, PIECE, 128)

    def factor(number):
        l = lax.broadcasted_iota(jnp.int32, (OWNED, 128), 1)
        i = lax.broadcasted_iota(jnp.int32, (OWNED, 128), 0)
        at_lane = jnp.where(i < PIECE, i, i - PIECE + UNIT) + 32 * number
        row = jnp.broadcast_to(factors[...], (NZ, OWNED, 128))
        return jnp.sum(jnp.where((l == at_lane)[None], row, 0.0), axis=2, keepdims=True)

    first_head = lax.broadcasted_iota(jnp.int32, (2 * COLS, 128), 1) < E

    def by_head(x):
        return jnp.where(first_head, x[: 2 * COLS], x[2 * COLS :])

    def product(pair, tile, first, count):
        probs = pfull[:, :, pl.ds(tile * 128, -(-count // 128) * 128)].reshape(NP * 128, -1)
        probs = probs[pair * 128 : (pair + 1) * 128, :count]
        return jnp.dot(probs, vp[pair, pl.ds(first, count), :], preferred_element_type=F32)

    def attend(number, tile, first, count):
        for pair in range(NP):
            whole = product(pair, tile, first, count)
            for row in range(ROWS):
                cut = slice(row * 128, (row + 1) * 128)
                parts[number, pair, :, cut] = by_head(whole[:, cut])

    for part in (2, 3, 0, 1):
        send(O, part, right, L)
    for part in (3, 2, 1, 0):
        send(O, part, left, R)
    for part in range(4):
        send(O, part, across, Y)
    for part in range(4):
        hand_on(O, part)

    for copy in loads[:4]:
        copy.wait()
    project_q(0)
    from_mate(O)
    project_q(1)
    project_kv(O)
    take(L, 2)
    send(L, 2, right, OPP)
    take(R, 3)
    send(R, 3, left, OPP)
    logits(O)
    take(L, 3)
    take(R, 2)
    for part in (2, 3):
        send(L, part, across, YL)
    take(Y, 0, 1)
    for part in (0, 1):
        send(Y, part, right, YL)
    for part in (1, 0):
        send(Y, part, left, YR)
    take(L, 0)
    send(L, 0, right, OPP)
    take(R, 1)
    send(R, 1, left, OPP)
    take(Y, 2)
    take(L, 1)
    take(R, 0)
    take(Y, 3)
    from_mate(L)
    project_kv(L)
    send(R, 2, across, YR)
    logits(L)
    from_mate(R)
    project_kv(R)
    logits(R)
    take(OPP, 2, 3)
    from_mate(Y)
    project_kv(Y)
    logits(Y)
    take(YL, 0)
    send(YL, 0, right, YOPP)
    take(YR, 1, 2)
    send(YR, 1, left, YOPP)
    take(YL, 2, 3)
    fold(O)
    fold(L)
    send(R, 3, across, YR)
    take(YL, 1)
    fold(R)
    take(YR, 0)
    fold(Y)
    for part in (2, 3):
        send(OPP, part, across, YOPP)
    from_mate(YL)
    project_kv(YL)
    logits(YL)
    take(YR, 3)
    take(OPP, 0, 1)
    absorb(O, Y, L, R)
    spread(O, 2, 0)
    from_mate(YR)
    project_kv(YR)
    logits(YR)
    from_mate(OPP)
    project_kv(OPP)
    logits(OPP)
    take(YOPP, 2, 3)
    take(YOPP, 0, 1)
    project_part(YOPP, 0, 1)
    project_part(YOPP, 0, 0)
    from_mate(YOPP, 1)
    project_part(YOPP, 1, 1)
    from_mate(YOPP, 0)
    project_part(YOPP, 1, 0)
    logits(YOPP)

    fold(YL)
    fold(YR)
    project_kv(YOPP, late)
    shared(O, 2, 0)
    unpack(O, Y, 0)
    fold(OPP)
    spread(L, 2, 1)
    absorb(YL, YR, OPP)
    spread(YL, 3, 2)
    fold(YOPP)
    finish(YOPP)
    shared(L, 2, 1)
    unpack(L, R, 1)
    attend(0, 0, O * UNIT, 4 * UNIT)
    shared(YL, 3, 2)
    unpack(YL, YR, 2)
    unpack(OPP, OPP, 3)
    attend(1, 2, YL * UNIT, 3 * UNIT)
    group(factors.at[pl.ds(0, NZ - 1)], ftx_sem, frx_sem).wait_recv()
    scaling = [factor(number).reshape(NP * 128, 1) for number in range(2)]
    shared(YOPP, 1, 3)
    unpack(YOPP, YOPP, 4)

    handed = []
    for pair in range(NP):
        lanes = pl.ds(pair * 128, 128)
        last = product(pair, 4, YOPP * UNIT, UNIT)
        ranks = [by_head(jnp.broadcast_to(f[pair * 128 : (pair + 1) * 128], (128, 128))) for f in scaling]
        for row in range(ROWS):
            cut = slice(row * 128, (row + 1) * 128)
            picked = by_head(last[:, cut])
            for number, rank in enumerate(ranks):
                picked = picked + rank * parts[number, pair, :, cut]
            picked = picked.astype(BF16)
            full[row, :, lanes] = picked[:COLS]
            half[pair, row] = picked[COLS:]
        copy = pltpu.make_async_remote_copy(
            src_ref=half.at[pair],
            dst_ref=full.at[:, :, pl.ds(HD + pair * 128, 128)],
            send_sem=htx_sem.at[pair],
            recv_sem=hrx_sem.at[pair],
            device_id=mate,
            device_id_type=MESH,
        )
        copy.start()
        handed.append(copy)
    for copy in loads[4:]:
        copy.wait()
    for copy in handed:
        copy.wait_recv()
    mixed = jnp.dot(full[...].reshape(ROWS * COLS, D), wo[...], preferred_element_type=F32)
    out_ref[...] = mixed.astype(BF16).reshape(ROWS, COLS, D)

    for count, way in ((7, 0), (8, 1)):
        ref = xs.at[pl.ds(0, count), 0]
        pltpu.make_async_remote_copy(
            src_ref=ref,
            dst_ref=ref,
            send_sem=tx_sem.at[way],
            recv_sem=mate_sem.at[0, 0],
            device_id=mate,
            device_id_type=MESH,
        ).wait_send()
    group(rz.at[:, pl.ds(0, NZ - 1)], ltx_sem, lrx_sem.at[0]).wait_send()
    group(sz, ytx_sem, yrx_sem.at[0]).wait_send()
    group(pall.at[pl.ds(0, NZ - 1)], ptx_sem, prx_sem.at[0]).wait_send()
    group(factors.at[pl.ds(0, NZ - 1)], ftx_sem, frx_sem).wait_send()
    for copy in handed:
        copy.wait_send()


def body(alignment_embedding, probe_projector, lookup_projector, content_projector, final_projector):
    hbm = pl.BlockSpec(memory_space=pl.ANY)
    return pl.pallas_call(
        kernel,
        out_shape=jax.ShapeDtypeStruct((ROWS, COLS, D), BF16),
        in_specs=[hbm] * 5,
        out_specs=pl.BlockSpec(memory_space=pltpu.VMEM),
        scratch_shapes=[
            pltpu.VMEM((8, 2, ROWS, COLS, D), BF16),
            pltpu.VMEM((D, HD), BF16),
            pltpu.VMEM((D, D), BF16),
            pltpu.VMEM((D, D), BF16),
            pltpu.VMEM((NP, 4 * COLS, ROWS * 128), BF16),
            pltpu.VMEM((NP, SITES, ROWS * 128), BF16),
            pltpu.VMEM((NP, SITES, ROWS * 128), BF16),
            pltpu.VMEM((8, NZ, PIECE, 128), F32),
            pltpu.VMEM((NP * 128, 128), F32),
            pltpu.VMEM((8, NZ, PIECE, 128), F32),
            pltpu.VMEM((8, PIECE, 128), F32),
            pltpu.VMEM((8, PIECE, 128), F32),
            pltpu.VMEM((NZ, 8, PIECE, 128), BF16),
            pltpu.VMEM((NZ, 1, 128), F32),
            pltpu.VMEM((NZ, OWNED, SITES + 128), BF16),
            pltpu.VMEM((2, NP, 2 * COLS, ROWS * 128), F32),
            pltpu.VMEM((NP, ROWS, COLS, 128), BF16),
            pltpu.VMEM((ROWS, COLS, D), BF16),
            pltpu.SemaphoreType.DMA((6,)),
            pltpu.SemaphoreType.DMA((2,)),
            pltpu.SemaphoreType.DMA((8, 4)),
            pltpu.SemaphoreType.DMA((8, 2)),
            pltpu.SemaphoreType.DMA,
            pltpu.SemaphoreType.DMA((8,)),
            pltpu.SemaphoreType.DMA,
            pltpu.SemaphoreType.DMA((8,)),
            pltpu.SemaphoreType.DMA,
            pltpu.SemaphoreType.DMA((4,)),
            pltpu.SemaphoreType.DMA,
            pltpu.SemaphoreType.DMA,
            pltpu.SemaphoreType.DMA((NP,)),
            pltpu.SemaphoreType.DMA((NP,)),
        ],
        compiler_params=pltpu.CompilerParams(
            collective_id=0, has_side_effects=True, vmem_limit_bytes=53 * 2**20
        ),
        name="tied_rows",
    )(
        alignment_embedding,
        probe_projector,
        lookup_projector,
        content_projector,
        final_projector,
    )


def solution(mesh):
    placed = (P("seq", "res", None), P(), P(), P(), P())
    return jax.shard_map(
        body, mesh=mesh, in_specs=placed, out_specs=P("seq", "res", None), check_vma=False
    )
```

```python
import math

import jax
import jax.numpy as jnp
from jax import lax
from jax.experimental import pallas as pl
from jax.experimental.pallas import tpu as pltpu
from jax.sharding import PartitionSpec as P

MESH = pl.DeviceIdType.MESH
BF16, F32 = jnp.bfloat16, jnp.float32

H = 12
E = 64
D = 768
ROWS = 16
COLS = 32
NSEQ = 16
HD = D // 2
NP = HD // 128
SITES = 512

O, Y, L, R, YL, YR, OPP, YOPP = range(8)
PARTS = {b: ((0, 5), (5, 4), (9, 3), (12, 4)) for b in range(8)}
PARTS[YOPP] = ((0, 5), (5, 5), (10, 3), (13, 3))
UNIT = 2 * COLS
NZ = 8
OWNED = HD * UNIT // E // NZ
PIECE = OWNED // 2


def kernel(
    x_hbm,
    wq_hbm,
    wk_hbm,
    wv_hbm,
    wo_hbm,
    out_ref,
    xs,
    wq,
    wkv,
    wo,
    qp,
    kp,
    vp,
    ls,
    lbuf,
    rz,
    sz,
    ry,
    pall,
    factors,
    pfull,
    parts,
    half,
    full,
    in_sem,
    tx_sem,
    rx_sem,
    mate_sem,
    ltx_sem,
    lrx_sem,
    ytx_sem,
    yrx_sem,
    ptx_sem,
    prx_sem,
    ftx_sem,
    frx_sem,
    htx_sem,
    hrx_sem,
):
    s, r = lax.axis_index("seq"), lax.axis_index("res")
    z, yl = s // 2, lax.rem(s, 2)
    ix, yh, core = r // 4, lax.rem(r // 2, 2), lax.rem(r, 2)

    def at(dx, dy, dc):
        return (s, lax.rem(ix + dx + 4, 4) * 4 + lax.rem(yh + dy, 2) * 2 + lax.rem(core + dc, 2))

    right, left, across, mate = at(1, 0, 0), at(-1, 0, 0), at(0, 1, 0), at(0, 0, 1)

    def far_first(k):
        return 4 + (k + 1) // 2 * (1 - 2 * lax.rem(k, 2))

    def above(d):
        return (lax.rem(z + d, NZ) * 2 + yl, r)

    twin = (z * 2 + 1 - yl, r)

    barrier = pltpu.get_barrier_semaphore()
    for device in (right, left, across, mate, twin, *(above(d) for d in range(1, NZ))):
        pl.semaphore_signal(barrier, inc=1, device_id=device, device_id_type=MESH)

    mine = pl.ds(pl.multiple_of(core * HD, HD), HD)
    others = pl.ds(pl.multiple_of((1 - core) * HD, HD), HD)
    loads = [
        pltpu.make_async_copy(x_hbm, xs.at[O, 0], in_sem.at[0]),
        pltpu.make_async_copy(wq_hbm.at[:, mine], wq, in_sem.at[1]),
        pltpu.make_async_copy(wk_hbm.at[:, mine], wkv.at[:, pl.ds(0, HD)], in_sem.at[2]),
        pltpu.make_async_copy(wv_hbm.at[:, mine], wkv.at[:, pl.ds(HD, HD)], in_sem.at[3]),
        pltpu.make_async_copy(wo_hbm.at[mine, :], wo.at[pl.ds(0, HD)], in_sem.at[4]),
        pltpu.make_async_copy(wo_hbm.at[others, :], wo.at[pl.ds(HD, HD)], in_sem.at[5]),
    ]
    for copy in loads:
        copy.start()
    pl.semaphore_wait(barrier, 5 + NZ - 1)

    def send(block, part, device, landing):
        rows = pl.ds(*PARTS[landing][part])
        pltpu.make_async_remote_copy(
            src_ref=x_hbm.at[rows] if block == O else xs.at[block, 0, rows],
            dst_ref=xs.at[landing, 0, rows],
            send_sem=tx_sem.at[0],
            recv_sem=rx_sem.at[landing, part],
            device_id=device,
            device_id_type=MESH,
        ).start()

    def hand_on(block, part):
        rows = pl.ds(*PARTS[block][part])
        pltpu.make_async_remote_copy(
            src_ref=x_hbm.at[rows] if block == O else xs.at[block, 0, rows],
            dst_ref=xs.at[block, 1, rows],
            send_sem=tx_sem.at[1],
            recv_sem=mate_sem.at[block, part // 2],
            device_id=mate,
            device_id_type=MESH,
        ).start()

    def received(ref, recv_sem):
        return pltpu.make_async_remote_copy(
            src_ref=ref,
            dst_ref=ref,
            send_sem=tx_sem.at[0],
            recv_sem=recv_sem,
            device_id=mate,
            device_id_type=MESH,
        )

    def take(block, *parts):
        for part in parts:
            received(xs.at[block, 0, pl.ds(*PARTS[block][part])], rx_sem.at[block, part]).wait_recv()
            hand_on(block, part)

    def from_mate(block, *halves):
        for side in halves or (0, 1):
            (first, some), (_, more) = PARTS[block][2 * side : 2 * side + 2]
            ref = xs.at[block, 1, pl.ds(first, some + more)]
            received(ref, mate_sem.at[block, side]).wait_recv()

    def project_rows(block, cr, first, rows, pairs):
        x = xs[block, cr, pl.ds(first, rows)].reshape(rows * COLS, D)
        w = wkv[:, pl.ds(pairs[0] * 128, len(pairs) * 128)]
        y = jnp.dot(x, w, preferred_element_type=F32).astype(BF16)
        j = pl.ds(pl.multiple_of((2 * block + cr) * COLS, COLS), COLS)
        for row in range(rows):
            lanes = pl.ds((first + row) * 128, 128)
            for n, pair in enumerate(pairs):
                here = y[row * COLS : (row + 1) * COLS, n * 128 : (n + 1) * 128]
                if pair < NP:
                    kp[pair, j, lanes] = here
                else:
                    vp[pair - NP, j, lanes] = here

    def project_kv(block, pairs=range(2 * NP)):
        def one(cr, _):
            project_rows(block, cr, 0, ROWS, pairs)
            return 0

        lax.fori_loop(0, 2, one, 0)

    early, late = range(0, NP + 1), range(NP + 1, 2 * NP)

    def project_part(block, cr, side):
        (first, some), (_, more) = PARTS[block][2 * side : 2 * side + 2]
        project_rows(block, cr, first, some + more, early)

    def project_q(cr):
        x = xs[O, cr].reshape(ROWS * COLS, D)
        y = jnp.dot(x, wq[...], preferred_element_type=F32).astype(BF16)
        low = lax.broadcasted_iota(jnp.int32, (COLS, 128), 1) < E
        zero = jnp.zeros((COLS, 128), BF16)
        for row in range(ROWS):
            for pair in range(NP):
                q = y[row * COLS : (row + 1) * COLS, pair * 128 : (pair + 1) * 128]
                lanes = pl.ds(row * 128, 128)
                qp[pair, pl.ds(cr * COLS, COLS), lanes] = jnp.where(low, q, zero)
                qp[pair, pl.ds(2 * COLS + cr * COLS, COLS), lanes] = jnp.where(low, zero, q)

    low = lax.broadcasted_iota(jnp.int32, (PIECE, 128), 1) < UNIT

    def multiply(unit, first, rows, more=False):
        lanes = pl.ds(first * 128, rows * 128)
        for pair in range(NP):
            k = kp[pair, pl.ds(unit * UNIT, UNIT), lanes]
            part = lax.dot_general(
                qp[pair, :, lanes],
                jnp.concatenate([k, k], axis=0),
                (((1,), (1,)), ((), ())),
                preferred_element_type=F32,
            )
            here = pl.ds(pair * 128, 128)
            lbuf[here, :] = lbuf[here, :] + part if more else part

    def logits(unit, done=ROWS):
        multiply(unit, 0, done, done < ROWS)
        for owner in range(NZ):
            ls[unit, owner] = jnp.where(
                low,
                lbuf[pl.ds(owner * OWNED, PIECE), :],
                lbuf[pl.ds(owner * OWNED + PIECE, PIECE), :],
            )

        def along_z(k, _):
            to = lax.rem(z + far_first(k), NZ)
            pltpu.make_async_remote_copy(
                src_ref=ls.at[unit, to],
                dst_ref=rz.at[unit, z],
                send_sem=ltx_sem,
                recv_sem=lrx_sem.at[unit],
                device_id=(to * 2 + yl, r),
                device_id_type=MESH,
            ).start()
            return 0

        lax.fori_loop(0, NZ - 1, along_z, 0)
        rz[unit, z] = ls[unit, z]

    scale = 1.0 / math.sqrt(E * ROWS * NSEQ)

    def group(ref, send_sem, recv_sem):
        return pltpu.make_async_remote_copy(
            src_ref=ref,
            dst_ref=ref,
            send_sem=send_sem,
            recv_sem=recv_sem,
            device_id=mate,
            device_id_type=MESH,
        )

    def fold(unit):
        group(rz.at[unit, pl.ds(0, NZ - 1)], ltx_sem, lrx_sem.at[unit]).wait_recv()
        sz[unit] = jnp.sum(rz[unit], axis=0)
        pltpu.make_async_remote_copy(
            src_ref=sz.at[unit],
            dst_ref=ry.at[unit],
            send_sem=ytx_sem,
            recv_sem=yrx_sem.at[unit],
            device_id=twin,
            device_id_type=MESH,
        ).start()

    def halves(reduce, x, fill):
        first = reduce(jnp.where(low, x, fill), axis=1, keepdims=True)
        second = reduce(jnp.where(low, fill, x), axis=1, keepdims=True)
        return jnp.where(low, first, second)

    def scores_of(unit):
        group(ry.at[unit], ytx_sem, yrx_sem.at[unit]).wait_recv()
        return (sz[unit] + ry[unit]) * scale

    stats = []

    def absorb(*units):
        scores = [scores_of(unit) for unit in units]
        top = scores[0]
        for other in scores[1:]:
            top = jnp.maximum(top, other)
        top = halves(jnp.max, top, -jnp.inf)
        total = jnp.zeros((PIECE, 128), F32)
        for unit, score in zip(units, scores):
            weights = jnp.exp(score - top)
            total = total + weights
            pall[z, unit] = weights.astype(BF16)
        stats.append((top, halves(jnp.sum, total, 0.0)))

    def to_line(ref, send_sem, recv_sem):
        def one(k, _):
            pltpu.make_async_remote_copy(
                src_ref=ref,
                dst_ref=ref,
                send_sem=send_sem,
                recv_sem=recv_sem,
                device_id=above(far_first(k)),
                device_id_type=MESH,
            ).start()
            return 0

        lax.fori_loop(0, NZ - 1, one, 0)

    def spread(first, count, number):
        to_line(pall.at[z, pl.ds(first, count)], ptx_sem, prx_sem.at[number])

    def shared(first, count, number):
        ref = pall.at[pl.ds(0, NZ - 1), pl.ds(first, count)]
        group(ref, ptx_sem, prx_sem.at[number]).wait_recv()

    lane = lax.broadcasted_iota(jnp.int32, (PIECE, 128), 1)
    row_of = lax.broadcasted_iota(jnp.int32, (PIECE, 128), 0)

    def finish(unit):
        scores = scores_of(unit)
        top = halves(jnp.max, scores, -jnp.inf)
        for earlier, _ in stats:
            top = jnp.maximum(top, earlier)
        weights = jnp.exp(scores - top)
        total = halves(jnp.sum, weights, 0.0)
        scales = [jnp.exp(earlier - top) for earlier, _ in stats]
        for earlier, (_, part) in zip(scales, stats):
            total = total + earlier * part
        pall[z, unit] = (weights / total).astype(BF16)
        spread(unit, 1, 3)
        placed = jnp.zeros((PIECE, 128), F32)
        for number, earlier in enumerate(scales):
            here = lax.rem(lane, UNIT) == row_of + 32 * number
            placed = jnp.where(here, earlier / total, placed)
        factors[z] = jnp.sum(placed, axis=0, keepdims=True)
        to_line(factors.at[z], ftx_sem, frx_sem)

    def unpack(left_unit, right_unit, tile):
        even, odd = (
            pall[:, u].astype(F32).reshape(NZ * PIECE, 128) for u in (left_unit, right_unit)
        )
        wide = lax.broadcasted_iota(jnp.int32, (NZ * PIECE, 128), 1) < UNIT
        first = jnp.where(wide, even, pltpu.roll(odd, UNIT, 1))
        second = jnp.where(wide, pltpu.roll(even, UNIT, 1), odd)
        lanes = pl.ds(tile * 128, 128)
        for n, rows in enumerate((first, second)):
            pfull[:, pl.ds(n * PIECE, PIECE), lanes] = rows.astype(BF16).reshape(NZ, PIECE, 128)

    def factor(number):
        l = lax.broadcasted_iota(jnp.int32, (OWNED, 128), 1)
        i = lax.broadcasted_iota(jnp.int32, (OWNED, 128), 0)
        at_lane = jnp.where(i < PIECE, i, i - PIECE + UNIT) + 32 * number
        row = jnp.broadcast_to(factors[...], (NZ, OWNED, 128))
        return jnp.sum(jnp.where((l == at_lane)[None], row, 0.0), axis=2, keepdims=True)

    first_head = lax.broadcasted_iota(jnp.int32, (2 * COLS, 128), 1) < E

    def by_head(x):
        return jnp.where(first_head, x[: 2 * COLS], x[2 * COLS :])

    def product(pair, tile, first, count):
        probs = pfull[:, :, pl.ds(tile * 128, -(-count // 128) * 128)].reshape(NP * 128, -1)
        probs = probs[pair * 128 : (pair + 1) * 128, :count]
        return jnp.dot(probs, vp[pair, pl.ds(first, count), :], preferred_element_type=F32)

    def attend(number, tile, first, count):
        for pair in range(NP):
            whole = product(pair, tile, first, count)
            for row in range(ROWS):
                cut = slice(row * 128, (row + 1) * 128)
                parts[number, pair, :, cut] = by_head(whole[:, cut])

    for part in (2, 3, 0, 1):
        send(O, part, right, L)
    for part in (3, 2, 1, 0):
        send(O, part, left, R)
    for part in range(4):
        send(O, part, across, Y)
    for part in range(4):
        hand_on(O, part)

    for copy in loads[:4]:
        copy.wait()
    project_q(0)
    from_mate(O)
    project_q(1)
    project_kv(O)
    take(L, 2)
    send(L, 2, right, OPP)
    take(R, 3)
    send(R, 3, left, OPP)
    logits(O)
    take(L, 3)
    take(R, 2)
    for part in (2, 3):
        send(L, part, across, YL)
    take(Y, 0, 1)
    for part in (0, 1):
        send(Y, part, right, YL)
    for part in (1, 0):
        send(Y, part, left, YR)
    take(L, 0)
    send(L, 0, right, OPP)
    take(R, 1)
    send(R, 1, left, OPP)
    take(Y, 2)
    take(L, 1)
    take(R, 0)
    take(Y, 3)
    from_mate(L)
    project_kv(L)
    send(R, 2, across, YR)
    logits(L)
    from_mate(R)
    project_kv(R)
    logits(R)
    take(OPP, 2, 3)
    from_mate(Y)
    project_kv(Y)
    logits(Y)
    take(YL, 0)
    send(YL, 0, right, YOPP)
    take(YR, 1, 2)
    send(YR, 1, left, YOPP)
    take(YL, 2, 3)
    fold(O)
    fold(L)
    send(R, 3, across, YR)
    take(YL, 1)
    fold(R)
    take(YR, 0)
    fold(Y)
    for part in (2, 3):
        send(OPP, part, across, YOPP)
    from_mate(YL)
    project_kv(YL)
    logits(YL)
    take(YR, 3)
    take(OPP, 0, 1)
    absorb(O, Y, L, R)
    spread(O, 2, 0)
    from_mate(YR)
    project_kv(YR)
    logits(YR)
    from_mate(OPP)
    project_kv(OPP)
    logits(OPP)
    take(YOPP, 2, 3)
    take(YOPP, 0, 1)
    project_part(YOPP, 0, 1)
    project_part(YOPP, 0, 0)
    from_mate(YOPP, 1)
    project_part(YOPP, 1, 1)
    split = PARTS[YOPP][2][0]
    multiply(YOPP, split, ROWS - split)
    from_mate(YOPP, 0)
    project_part(YOPP, 1, 0)
    logits(YOPP, split)

    fold(YL)
    fold(YR)
    project_kv(YOPP, late)
    shared(O, 2, 0)
    unpack(O, Y, 0)
    fold(OPP)
    spread(L, 2, 1)
    absorb(YL, YR, OPP)
    spread(YL, 3, 2)
    fold(YOPP)
    finish(YOPP)
    shared(L, 2, 1)
    unpack(L, R, 1)
    attend(0, 0, O * UNIT, 4 * UNIT)
    shared(YL, 3, 2)
    unpack(YL, YR, 2)
    unpack(OPP, OPP, 3)
    attend(1, 2, YL * UNIT, 3 * UNIT)
    shared(YOPP, 1, 3)
    unpack(YOPP, YOPP, 4)
    group(factors.at[pl.ds(0, NZ - 1)], ftx_sem, frx_sem).wait_recv()
    scaling = [factor(number).reshape(NP * 128, 1) for number in range(2)]

    handed = []
    for pair in range(NP):
        lanes = pl.ds(pair * 128, 128)
        last = product(pair, 4, YOPP * UNIT, UNIT)
        ranks = [by_head(jnp.broadcast_to(f[pair * 128 : (pair + 1) * 128], (128, 128))) for f in scaling]
        for row in range(ROWS):
            cut = slice(row * 128, (row + 1) * 128)
            picked = by_head(last[:, cut])
            for number, rank in enumerate(ranks):
                picked = picked + rank * parts[number, pair, :, cut]
            picked = picked.astype(BF16)
            full[row, :, lanes] = picked[:COLS]
            half[pair, row] = picked[COLS:]
        copy = pltpu.make_async_remote_copy(
            src_ref=half.at[pair],
            dst_ref=full.at[:, :, pl.ds(HD + pair * 128, 128)],
            send_sem=htx_sem.at[pair],
            recv_sem=hrx_sem.at[pair],
            device_id=mate,
            device_id_type=MESH,
        )
        copy.start()
        handed.append(copy)
    for copy in loads[4:]:
        copy.wait()
    for copy in handed:
        copy.wait_recv()
    mixed = jnp.dot(full[...].reshape(ROWS * COLS, D), wo[...], preferred_element_type=F32)
    out_ref[...] = mixed.astype(BF16).reshape(ROWS, COLS, D)

    for count, way in ((7, 0), (8, 1)):
        ref = xs.at[pl.ds(0, count), 0]
        pltpu.make_async_remote_copy(
            src_ref=ref,
            dst_ref=ref,
            send_sem=tx_sem.at[way],
            recv_sem=mate_sem.at[0, 0],
            device_id=mate,
            device_id_type=MESH,
        ).wait_send()
    group(rz.at[:, pl.ds(0, NZ - 1)], ltx_sem, lrx_sem.at[0]).wait_send()
    group(sz, ytx_sem, yrx_sem.at[0]).wait_send()
    group(pall.at[pl.ds(0, NZ - 1)], ptx_sem, prx_sem.at[0]).wait_send()
    group(factors.at[pl.ds(0, NZ - 1)], ftx_sem, frx_sem).wait_send()
    for copy in handed:
        copy.wait_send()


def body(alignment_embedding, probe_projector, lookup_projector, content_projector, final_projector):
    hbm = pl.BlockSpec(memory_space=pl.ANY)
    return pl.pallas_call(
        kernel,
        out_shape=jax.ShapeDtypeStruct((ROWS, COLS, D), BF16),
        in_specs=[hbm] * 5,
        out_specs=pl.BlockSpec(memory_space=pltpu.VMEM),
        scratch_shapes=[
            pltpu.VMEM((8, 2, ROWS, COLS, D), BF16),
            pltpu.VMEM((D, HD), BF16),
            pltpu.VMEM((D, D), BF16),
            pltpu.VMEM((D, D), BF16),
            pltpu.VMEM((NP, 4 * COLS, ROWS * 128), BF16),
            pltpu.VMEM((NP, SITES, ROWS * 128), BF16),
            pltpu.VMEM((NP, SITES, ROWS * 128), BF16),
            pltpu.VMEM((8, NZ, PIECE, 128), F32),
            pltpu.VMEM((NP * 128, 128), F32),
            pltpu.VMEM((8, NZ, PIECE, 128), F32),
            pltpu.VMEM((8, PIECE, 128), F32),
            pltpu.VMEM((8, PIECE, 128), F32),
            pltpu.VMEM((NZ, 8, PIECE, 128), BF16),
            pltpu.VMEM((NZ, 1, 128), F32),
            pltpu.VMEM((NZ, OWNED, SITES + 128), BF16),
            pltpu.VMEM((2, NP, 2 * COLS, ROWS * 128), F32),
            pltpu.VMEM((NP, ROWS, COLS, 128), BF16),
            pltpu.VMEM((ROWS, COLS, D), BF16),
            pltpu.SemaphoreType.DMA((6,)),
            pltpu.SemaphoreType.DMA((2,)),
            pltpu.SemaphoreType.DMA((8, 4)),
            pltpu.SemaphoreType.DMA((8, 2)),
            pltpu.SemaphoreType.DMA,
            pltpu.SemaphoreType.DMA((8,)),
            pltpu.SemaphoreType.DMA,
            pltpu.SemaphoreType.DMA((8,)),
            pltpu.SemaphoreType.DMA,
            pltpu.SemaphoreType.DMA((4,)),
            pltpu.SemaphoreType.DMA,
            pltpu.SemaphoreType.DMA,
            pltpu.SemaphoreType.DMA((NP,)),
            pltpu.SemaphoreType.DMA((NP,)),
        ],
        compiler_params=pltpu.CompilerParams(
            collective_id=0, has_side_effects=True, vmem_limit_bytes=53 * 2**20
        ),
        name="tied_rows",
    )(
        alignment_embedding,
        probe_projector,
        lookup_projector,
        content_projector,
        final_projector,
    )


def solution(mesh):
    placed = (P("seq", "res", None), P(), P(), P(), P())
    return jax.shard_map(
        body, mesh=mesh, in_specs=placed, out_specs=P("seq", "res", None), check_vma=False
    )
```
